32 devices in a mesh: slab: 2 (over x), shot: 8 (over z, y), rcv: 2 (over core).
Axes of the slice: x: 2, y: 2, z: 4, core: 2. Of those that a mesh axis runs over, the one named last changes fastest.
Arguments:
- traces: bfloat16 [16, 256, 1536], P(('slab', 'shot'), 'rcv'), parts along dimension 0, may hold values from -6 to 6
- rcv_delay: int32 [16, 256, 9], P(('slab', 'shot'), 'rcv'), parts along dimension 0, may hold values from 0 to 47
- rcv_frac: int32 [16, 256, 9], P(('slab', 'shot'), 'rcv'), parts along dimension 0, may hold values from 0 to 255
- live_count: int32 [16], P(('slab', 'shot')), parts along dimension 0, may hold values from 64 to 256
- src_delay: int32 [16, 2, 128, 9], P('slab', 'rcv', 'shot'), parts along dimension 0, may hold values from 0 to 47
- src_frac: int32 [16, 2, 128, 9], P('slab', 'rcv', 'shot'), parts along dimension 0, may hold values from 0 to 255
- rcv_taper: float32 [9], replicated, may hold values from 0.5 to 1.5
- src_taper: float32 [9], replicated, may hold values from 0.5 to 1.5
Outputs:
- redatumed: bfloat16 [16, 2, 128, 1536], P('slab', 'rcv', 'shot'), parts along dimension 0
The draws below stay inside these ranges and needn't reach their ends.
There are 2 independent parts, one for each index of `slab`. The reference program is written for one: setup_inputs(seed, part) draws one part's arguments, and reference() takes and returns one part's arrays. A program takes and returns all parts, laid end to end along the dimension named above; an argument that names none is the same for every part. Nothing has to cross between parts.
All inputs are finite; a program needn't handle non-finite values.
Results may differ from the reference program's by a relative error of at most 0.0055.
Values may be sent and summed in bfloat16 or wider, within the bound.
A program may use at most 64 MiB of HBM per device.

```python
import jax
import jax.numpy as jnp

NT = 1536
NR = 256
AR = 4
AS = 4
TRI = 2
DMAX = 48
KR = 9
KS = 9
NS = 8
N_RCV = 2


def set_ends(drawn, key, low, high):
    longest = drawn.shape.index(max(drawn.shape))
    spots = []
    for shift in (0, 1):
        where = [jax.random.randint(jax.random.fold_in(key, axis), (), 0, length) for axis, length in enumerate(drawn.shape)]
        where[longest] = (where[longest] + shift) % drawn.shape[longest]
        spots.append(tuple(where))
    return drawn.at[spots[0]].set(low).at[spots[1]].set(high)


def shard_levels(key, extent, cuts, low, high):
    factor_of = 1.0
    for dim, shards_of in cuts:
        heights = jax.random.uniform(jax.random.fold_in(jax.random.fold_in(key, 6), dim), (shards_of,), jnp.float32, low / len(cuts), high / len(cuts))
        factor_of = factor_of * jnp.repeat(jnp.exp(heights), extent[dim] // shards_of).reshape((-1,) + (1,) * (len(extent) - 1 - dim))
    return factor_of


def normal_values(stream_key, extent, width, limit, cuts=(), held_as=jnp.bfloat16):
    level = shard_levels(stream_key, extent, cuts, -0.22, 0.18) if cuts else 1.0
    values = jax.random.normal(stream_key, extent, jnp.float32) * width * level
    return jnp.minimum(jnp.maximum(values, -limit), limit).astype(held_as)


def setup_inputs(seed: int = 0, part: int = 0) -> dict:
    keys = jax.random.split(jax.random.key(seed), 9)
    part_keys = jax.random.split(jax.random.fold_in(keys[8], part), 9)
    traces = normal_values(part_keys[0], (NS, NR, NT), 1.0, 6.0, ((0, 8), (1, 2)))
    rcv_delay = set_ends(jax.random.randint(part_keys[1], (NS, NR, KR), 0, DMAX), jax.random.fold_in(part_keys[1], 1), 0, DMAX - 1).astype(jnp.int32)
    rcv_frac = set_ends(jax.random.randint(part_keys[2], (NS, NR, KR), 0, 256), jax.random.fold_in(part_keys[2], 1), 0, 255).astype(jnp.int32)
    live_count = set_ends(jax.random.randint(part_keys[3], (NS,), NR // 4, NR + 1), jax.random.fold_in(part_keys[3], 1), NR // 4, NR).astype(jnp.int32)
    src_delay = set_ends(jax.random.randint(part_keys[4], (NS, N_RCV, NR // N_RCV, KS), 0, DMAX), jax.random.fold_in(part_keys[4], 1), 0, DMAX - 1).astype(jnp.int32)
    src_frac = set_ends(jax.random.randint(part_keys[5], (NS, N_RCV, NR // N_RCV, KS), 0, 256), jax.random.fold_in(part_keys[5], 1), 0, 255).astype(jnp.int32)
    rcv_taper = jnp.clip(jax.random.uniform(keys[6], (KR,), jnp.float32, 0.5, 1.5), 0.5, 1.5)
    src_taper = jnp.clip(jax.random.uniform(keys[7], (KS,), jnp.float32, 0.5, 1.5), 0.5, 1.5)
    return dict(traces=traces, rcv_delay=rcv_delay, rcv_frac=rcv_frac, live_count=live_count, src_delay=src_delay, src_frac=src_frac, rcv_taper=rcv_taper, src_taper=src_taper)


def triangle_matrix():
    rows = jnp.arange(NT, dtype=jnp.int32)[:, None]
    cols = jnp.arange(NT, dtype=jnp.int32)[None, :]
    height = jnp.maximum(TRI - jnp.abs(cols - rows), 0).astype(jnp.float32)
    energy = jnp.sum(jnp.maximum(TRI - jnp.abs(jnp.arange(-TRI, TRI + 1, dtype=jnp.int32)), 0).astype(jnp.float32) ** 2)
    return (height / jnp.sqrt(energy)).astype(jnp.bfloat16)

def apply_filter(block, matrix):
    flat = block.reshape(-1, NT)
    return jnp.dot(flat, matrix, preferred_element_type=jnp.float32).astype(jnp.bfloat16).reshape(block.shape)

def read_shifted(source, delay, frac):
    padded = jnp.pad(source, [(0, 0)] * (source.ndim - 1) + [(0, DMAX + 1)])
    index = jnp.arange(NT, dtype=jnp.int32) + delay[..., None].astype(jnp.int32)
    first = jnp.take_along_axis(padded, index, axis=-1).astype(jnp.float32)
    second = jnp.take_along_axis(padded, index + 1, axis=-1).astype(jnp.float32)
    weight = frac[..., None].astype(jnp.float32) / 256.0
    return (1.0 - weight) * first + weight * second

def reference(traces, rcv_delay, rcv_frac, live_count, src_delay, src_frac, rcv_taper, src_taper):
    matrix = triangle_matrix()
    filtered = apply_filter(traces, matrix)
    padded = jnp.pad(filtered, ((0, 0), (AR, AR), (0, 0)))
    total = jnp.zeros(traces.shape, jnp.float32)
    fold = jnp.zeros(traces.shape[:2], jnp.float32)
    for tap in range(KR):
        source = padded[:, tap:tap + NR, :]
        where = jnp.arange(NR, dtype=jnp.int32) + tap - AR
        live = ((where >= 0) & (where < NR))[None, :] & (where[None, :] < live_count[:, None])
        live = live.astype(jnp.float32)
        total = total + rcv_taper[tap] * live[..., None] * read_shifted(source, rcv_delay[:, :, tap], rcv_frac[:, :, tap])
        fold = fold + live
    section_one = (total / jnp.sqrt(jnp.maximum(fold, 1.0))[..., None]).astype(jnp.bfloat16)
    second = apply_filter(section_one, matrix)
    spaced = jnp.pad(second, ((AS, AS), (0, 0), (0, 0)))
    delay_two = src_delay.reshape(NS, NR, KS)
    frac_two = src_frac.reshape(NS, NR, KS)
    result = jnp.zeros(traces.shape, jnp.float32)
    count = jnp.zeros((NS,), jnp.float32)
    for tap in range(KS):
        source = spaced[tap:tap + NS]
        where = jnp.arange(NS, dtype=jnp.int32) + tap - AS
        inside = ((where >= 0) & (where < NS)).astype(jnp.float32)
        result = result + src_taper[tap] * inside[:, None, None] * read_shifted(source, delay_two[:, :, tap], frac_two[:, :, tap])
        count = count + inside
    result = result / jnp.sqrt(count)[:, None, None]
    return result.astype(jnp.bfloat16).reshape(NS, N_RCV, NR // N_RCV, NT)
```

```python
import functools

import jax
import jax.numpy as jnp
import numpy as np
from jax import lax
from jax.experimental import pallas as pl
from jax.experimental.pallas import tpu as pltpu
from jax.sharding import PartitionSpec as P

AR = 4
AS = 4
TRI = 2
LANES = 128
GROUP = 8
EDGE = 16
MESH = pl.DeviceIdType.MESH


def taps_of_filter():
    heights = np.maximum(TRI - np.abs(np.arange(-TRI, TRI + 1)), 0).astype(np.float32)
    taps = (heights / np.sqrt(np.sum(heights**2, dtype=np.float32))).astype(jnp.bfloat16)
    return [float(v) for v in taps[TRI:]]


MAIN_TAP, SIDE_TAP = taps_of_filter()[:2]


def ends(shape):
    lane = lax.broadcasted_iota(jnp.int32, shape, 1)
    return lane == 0, lane == LANES - 1


def smooth(raw):
    is_first, is_last = ends(raw[0].shape)
    zero = jnp.zeros_like(raw[0])
    up = [zero] + [pltpu.roll(x, 1, 1) for x in raw]
    down = [pltpu.roll(x, LANES - 1, 1) for x in raw] + [zero]
    done = []
    for b, x in enumerate(raw):
        before = jnp.where(is_first, up[b], up[b + 1])
        after = jnp.where(is_last, down[b + 1], down[b])
        done.append((MAIN_TAP * x + SIDE_TAP * (before + after)).astype(jnp.bfloat16))
    return done


def ahead(values):
    _, is_last = ends(values[0].shape)
    rolled = [pltpu.roll(x, LANES - 1, 1) for x in values] + [jnp.zeros_like(values[0])]
    return [jnp.where(is_last, rolled[b + 1], rolled[b]) for b in range(len(values))]


def gathered(idx, own, mixed, nb):
    now = mixed(0)
    for b in range(nb):
        after = mixed(b + 1) if b + 1 < nb else jnp.zeros_like(now)
        yield b, jnp.take_along_axis(jnp.where(own, now, after), idx, axis=1)
        now = after


def kernel(
    dims,
    live_hbm, rtaper_hbm, staper_hbm, x_hbm, rd_ref, rf_ref, sd_hbm, sf_hbm,
    out_ref,
    live_ref, rtaper_ref, staper_ref, x_ref, sd_ref, sf_ref, in_sem,
    flat, turned, near, near1, far, far1, halo, sec, got, acc,
    r_d, r_c0, r_c1, r_norm, t_d, t_c0, t_c1,
    halo_send, halo_recv, send_sem, recv_sem,
):
    rows, nt, peers, per_peer, n_rcv, kr, ks = dims
    nb = nt // LANES
    chunks = pl.cdiv(per_peer, GROUP)
    used = min(GROUP, per_peer)
    me = lax.axis_index("shot")
    side = lax.axis_index("rcv")
    other = 1 - side
    f32 = jnp.float32

    pairs = (
        (x_hbm.at[0], x_ref), (live_hbm, live_ref), (rtaper_hbm, rtaper_ref),
        (staper_hbm, staper_ref), (sd_hbm, sd_ref), (sf_hbm, sf_ref),
    )
    loads = [pltpu.make_async_copy(a, b, in_sem.at[n]) for n, (a, b) in enumerate(pairs)]
    for load in loads:
        load.start()

    barrier = pltpu.get_barrier_semaphore()

    def greet(i, carry):
        to = lax.rem(me + i, peers)
        pl.semaphore_signal(barrier, inc=1, device_id={"shot": to}, device_id_type=MESH)
        return carry

    pl.semaphore_signal(barrier, inc=1, device_id={"rcv": other}, device_id_type=MESH)
    lax.fori_loop(1, peers, greet, 0)

    for b in range(nb):
        for start in (0, EDGE + rows):
            near[b, start : start + EDGE, :] = jnp.zeros((EDGE, LANES), f32)
            near1[b, start : start + EDGE, :] = jnp.zeros((EDGE, LANES), f32)
    flat[...] = jnp.zeros_like(flat)

    lane = lax.broadcasted_iota(jnp.int32, (GROUP, LANES), 1)
    sub = lax.broadcasted_iota(jnp.int32, (GROUP, LANES), 0)

    def spread(column):
        packed = jnp.broadcast_to(column, (GROUP, LANES))
        return packed >> 8, (packed & 255).astype(f32) * (1.0 / 256.0)

    loads[1].wait()
    loads[2].wait()
    live_count = live_ref[0]
    for block in range(rows // LANES):
        cols = slice(block * LANES, (block + 1) * LANES)
        for a in range(kr):
            flat[a : a + 1, :] = rd_ref[a, :, cols] * 256 + rf_ref[a, :, cols]
        turned[block] = jnp.transpose(flat[...], (1, 0))

    def receiver_tables(g, carry):
        at = pl.ds(pl.multiple_of(g * GROUP, GROUP), GROUP)
        columns = turned[g // (LANES // GROUP), pl.ds(pl.multiple_of(lax.rem(g, LANES // GROUP) * GROUP, GROUP), GROUP), :]
        where0 = side * rows + g * GROUP + sub - AR
        fold = jnp.zeros((GROUP, LANES), f32)
        for a in range(kr):
            d, weight = spread(columns[:, a : a + 1])
            where = where0 + a
            live = (where >= 0) & (where < rows * n_rcv) & (where < live_count)
            live = live.astype(f32)
            fold = fold + live
            scale = rtaper_ref[a] * live
            r_d[a, at, :] = d
            r_c0[a, at, :] = scale * (1.0 - weight)
            r_c1[a, at, :] = scale * weight
        r_norm[at, :] = 1.0 / jnp.sqrt(jnp.maximum(fold, 1.0))
        return carry

    lax.fori_loop(0, rows // GROUP, receiver_tables, 0)

    pl.semaphore_wait(barrier, peers)

    halo_copy = pltpu.make_async_remote_copy(
        src_ref=x_hbm.at[0, pl.ds(pl.multiple_of(other * (rows - EDGE), EDGE), EDGE), :],
        dst_ref=halo,
        send_sem=halo_send,
        recv_sem=halo_recv,
        device_id={"rcv": other},
        device_id_type=MESH,
    )
    halo_copy.start()

    def filter_rows(load, base):
        done = [v.astype(f32) for v in smooth([load(b).astype(f32) for b in range(nb)])]
        for b, (value, value1) in enumerate(zip(done, ahead(done))):
            near[b, pl.ds(base, EDGE), :] = value
            near1[b, pl.ds(base, EDGE), :] = value1

    def filter_own(g, carry):
        start = pl.multiple_of(g * EDGE, EDGE)
        filter_rows(lambda b: x_ref[pl.ds(start, EDGE), b * LANES : (b + 1) * LANES], EDGE + start)
        return carry

    loads[0].wait()
    lax.fori_loop(0, rows // EDGE, filter_own, 0)

    edge_peer = other * (peers - 1)

    def partner(i, sign):
        step = peers // 2 + (1 - 2 * lax.rem(i, 2)) * ((i + 1) // 2)
        return lax.rem(me + sign * step + 2 * peers, peers)

    def send_of(to):
        return pltpu.make_async_remote_copy(
            src_ref=sec.at[to],
            dst_ref=got.at[me],
            send_sem=send_sem.at[to],
            recv_sem=recv_sem.at[me],
            device_id={"shot": to},
            device_id_type=MESH,
        )

    def recv_of(origin):
        return pltpu.make_async_remote_copy(
            src_ref=sec.at[origin],
            dst_ref=got.at[origin],
            send_sem=send_sem.at[origin],
            recv_sem=recv_sem.at[origin],
            device_id={"shot": origin},
            device_id_type=MESH,
        )

    def receiver_step(i, carry):
        to = partner(i, 1)

        @pl.when(to == edge_peer)
        def _():
            halo_copy.wait_recv()
            filter_rows(
                lambda b: halo[:, b * LANES : (b + 1) * LANES],
                pl.multiple_of(other * (EDGE + rows), EDGE),
            )

        for c in range(chunks):
            row0 = to * per_peer + c * GROUP
            if per_peer % GROUP == 0:
                row0 = pl.multiple_of(row0, GROUP)
            at = pl.ds(row0, GROUP)
            total = [None] * nb
            for a in range(kr):
                d, c0, c1 = r_d[a, at, :], r_c0[a, at, :], r_c1[a, at, :]
                source = pl.ds(EDGE - AR + row0 + a, GROUP)

                def mixed(b):
                    return c0 * near[b, source, :] + c1 * near1[b, source, :]

                for b, value in gathered((lane + d) & (LANES - 1), lane >= d, mixed, nb):
                    total[b] = value if a == 0 else total[b] + value
            norm = r_norm[at, :]
            one = [(v * norm).astype(jnp.bfloat16).astype(f32) for v in total]
            for b, value in enumerate(smooth(one)):
                sec[to, c * GROUP : c * GROUP + used, b * LANES : (b + 1) * LANES] = value[:used]

        @pl.when(i < peers - 1)
        def _():
            send_of(to).start()

        return carry

    lax.fori_loop(0, peers, receiver_step, 0)

    for n in (3, 4, 5):
        loads[n].wait()
    group = LANES // EDGE

    def source_tables(g, carry):
        for kk in range(group):
            for a in range(ks):
                at = kk * EDGE + a
                flat[at : at + 1, :per_peer] = sd_ref[g * group + kk, a] * 256 + sf_ref[g * group + kk, a]
        turned[0] = jnp.transpose(flat[...], (1, 0))
        for kk in range(group):
            k = g * group + kk
            count = jnp.minimum(k + ks - AS, peers) - jnp.maximum(k - AS, 0)
            norm = 1.0 / jnp.sqrt(jnp.full((GROUP, LANES), count, jnp.int32).astype(f32))
            for c in range(chunks):
                at = slice(c * GROUP, c * GROUP + GROUP)
                columns = turned[0, at, :]
                for a in range(ks):
                    d, weight = spread(columns[:, kk * EDGE + a : kk * EDGE + a + 1])
                    scale = staper_ref[a] * norm
                    t_d[k, a, at, :] = d
                    t_c0[k, a, at, :] = scale * (1.0 - weight)
                    t_c1[k, a, at, :] = scale * weight
        return carry

    lax.fori_loop(0, peers // group, source_tables, 0)

    def clear(k, carry):
        for b in range(nb):
            acc[k, b] = jnp.zeros(acc.shape[2:], f32)
        return carry

    lax.fori_loop(0, peers, clear, 0)

    if per_peer < GROUP:
        for b in range(nb):
            far[b] = jnp.zeros(far.shape[1:], f32)
            far1[b] = jnp.zeros(far.shape[1:], f32)
    width = min(peers, ks)

    def shot_sum(p, block_of):
        done = [block_of(b).astype(f32) for b in range(nb)]
        for b, (value, value1) in enumerate(zip(done, ahead(done))):
            far[b, :per_peer, :] = value
            far1[b, :per_peer, :] = value1
        base = 0 if width == peers else jnp.minimum(jnp.maximum(p - AS, 0), peers - width)
        for kk in range(width):
            k = base + kk
            tap = p - k + AS
            a = jnp.minimum(jnp.maximum(tap, 0), ks - 1)
            inside = jnp.where(tap == a, 1.0, 0.0)
            for c in range(chunks):
                at = slice(c * GROUP, c * GROUP + GROUP)
                d, c0, c1 = t_d[k, a, at, :], t_c0[k, a, at, :] * inside, t_c1[k, a, at, :] * inside

                def mixed(b):
                    return c0 * far[b, at, :] + c1 * far1[b, at, :]

                for b, value in gathered((lane + d) & (LANES - 1), lane >= d, mixed, nb):
                    acc[k, b, at, :] += value

    shot_sum(me, lambda b: sec[me, :, b * LANES : (b + 1) * LANES])

    def source_step(i, carry):
        origin = partner(i, -1)
        recv_of(origin).wait_recv()
        shot_sum(origin, lambda b: got[origin, :, b * LANES : (b + 1) * LANES])
        return carry

    lax.fori_loop(0, peers - 1, source_step, 0)

    def finish(k, carry):
        for b in range(nb):
            out_ref[k, 0, :, b * LANES : (b + 1) * LANES] = acc[k, b, :per_peer, :].astype(jnp.bfloat16)
        return carry

    lax.fori_loop(0, peers, finish, 0)

    halo_copy.wait_send()

    def drain(i, carry):
        send_of(partner(i, 1)).wait_send()
        return carry

    lax.fori_loop(0, peers - 1, drain, 0)


def body(traces, rcv_delay, rcv_frac, live_count, src_delay, src_frac, rcv_taper, src_taper):
    _, rows, nt = traces.shape
    peers = lax.axis_size("shot")
    n_rcv = lax.axis_size("rcv")
    per_peer = rows // peers
    kr, ks = rcv_delay.shape[-1], src_delay.shape[-1]
    nb = nt // LANES
    tall = pl.cdiv(per_peer, GROUP) * GROUP
    rcv_delay, rcv_frac = (jnp.transpose(v, (2, 0, 1)) for v in (rcv_delay, rcv_frac))
    src_delay, src_frac = (jnp.transpose(v, (0, 3, 1, 2)) for v in (src_delay, src_frac))
    dims = (rows, nt, peers, per_peer, n_rcv, kr, ks)
    hbm, vmem = pl.BlockSpec(memory_space=pltpu.HBM), pl.BlockSpec(memory_space=pltpu.VMEM)
    keep = functools.partial(pltpu.with_memory_space_constraint, memory_space=pltpu.HBM)
    near = functools.partial(pltpu.with_memory_space_constraint, memory_space=pltpu.VMEM)
    f32, bf16, i32 = jnp.float32, jnp.bfloat16, jnp.int32
    extended = (nb, rows + 2 * EDGE, LANES)
    r_table = (kr, rows + GROUP, LANES)
    t_table = (peers, ks, tall, LANES)
    return pl.pallas_call(
        functools.partial(kernel, dims),
        name="redatum",
        out_shape=pltpu.VMEM((peers, 1, per_peer, nt), bf16),
        in_specs=[hbm] * 4 + [vmem] * 2 + [hbm] * 2,
        out_specs=pl.BlockSpec(memory_space=pltpu.VMEM),
        scratch_shapes=[
            pltpu.SMEM((1,), i32),
            pltpu.SMEM((kr,), f32),
            pltpu.SMEM((ks,), f32),
            pltpu.VMEM((rows, nt), bf16),
            pltpu.VMEM(src_delay.shape, i32),
            pltpu.VMEM(src_delay.shape, i32),
            pltpu.SemaphoreType.DMA((6,)),
            pltpu.VMEM((LANES, LANES), i32),
            pltpu.VMEM((rows // LANES, LANES, LANES), i32),
            pltpu.VMEM(extended, f32),
            pltpu.VMEM(extended, f32),
            pltpu.VMEM((nb, tall, LANES), f32),
            pltpu.VMEM((nb, tall, LANES), f32),
            pltpu.VMEM((EDGE, nt), bf16),
            pltpu.VMEM((peers, per_peer, nt), bf16),
            pltpu.VMEM((peers, per_peer, nt), bf16),
            pltpu.VMEM((peers, nb, tall, LANES), f32),
            pltpu.VMEM(r_table, i32),
            pltpu.VMEM(r_table, f32),
            pltpu.VMEM(r_table, f32),
            pltpu.VMEM(r_table[1:], f32),
            pltpu.VMEM(t_table, i32),
            pltpu.VMEM(t_table, f32),
            pltpu.VMEM(t_table, f32),
            pltpu.SemaphoreType.DMA,
            pltpu.SemaphoreType.DMA,
            pltpu.SemaphoreType.DMA((peers,)),
            pltpu.SemaphoreType.DMA((peers,)),
        ],
        compiler_params=pltpu.CompilerParams(
            collective_id=0, has_side_effects=True, vmem_limit_bytes=60 * 2**20
        ),
    )(
        live_count, keep(rcv_taper), keep(src_taper), keep(traces), near(rcv_delay), near(rcv_frac), keep(src_delay), keep(src_frac)
    )


def solution(mesh):
    return jax.shard_map(
        body,
        mesh=mesh,
        in_specs=(
            P(("slab", "shot"), "rcv", None),
            P(("slab", "shot"), "rcv", None),
            P(("slab", "shot"), "rcv", None),
            P(("slab", "shot")),
            P("slab", "rcv", "shot", None),
            P("slab", "rcv", "shot", None),
            P(),
            P(),
        ),
        out_specs=P("slab", "rcv", "shot", None),
        check_vma=False,
    )
```

```python
import functools

import jax
import jax.numpy as jnp
import numpy as np
from jax import lax
from jax.experimental import pallas as pl
from jax.experimental.pallas import tpu as pltpu
from jax.sharding import PartitionSpec as P

AR = 4
AS = 4
TRI = 2
LANES = 128
GROUP = 8
EDGE = 16
FULL = 32000.0
TINY = 1e-30
MESH = pl.DeviceIdType.MESH


def taps_of_filter():
    heights = np.maximum(TRI - np.abs(np.arange(-TRI, TRI + 1)), 0).astype(np.float32)
    taps = (heights / np.sqrt(np.sum(heights**2, dtype=np.float32))).astype(jnp.bfloat16)
    return [float(v) for v in taps[TRI:]]


MAIN_TAP, SIDE_TAP = taps_of_filter()[:2]


def ends(shape):
    lane = lax.broadcasted_iota(jnp.int32, shape, 1)
    return lane == 0, lane == LANES - 1


def smooth(raw):
    is_first, is_last = ends(raw[0].shape)
    zero = jnp.zeros_like(raw[0])
    up = [zero] + [pltpu.roll(x, 1, 1) for x in raw]
    down = [pltpu.roll(x, LANES - 1, 1) for x in raw] + [zero]
    done = []
    for b, x in enumerate(raw):
        before = jnp.where(is_first, up[b], up[b + 1])
        after = jnp.where(is_last, down[b + 1], down[b])
        done.append((MAIN_TAP * x + SIDE_TAP * (before + after)).astype(jnp.bfloat16))
    return done


def ahead(values):
    _, is_last = ends(values[0].shape)
    rolled = [pltpu.roll(x, LANES - 1, 1) for x in values] + [jnp.zeros_like(values[0])]
    return [jnp.where(is_last, rolled[b + 1], rolled[b]) for b in range(len(values))]


def words(values):
    pairs = len(values) // 2
    top = functools.reduce(jnp.maximum, [jnp.abs(v) for v in values])
    top = jnp.maximum(jnp.max(top, axis=1, keepdims=True), TINY)
    top = jnp.broadcast_to(top, values[0].shape)
    scale = FULL / top
    whole = [(v * scale).astype(jnp.int32) for v in values]
    packed = [(whole[b] << 16) + whole[b + pairs] for b in range(pairs)]
    return packed + [whole[pairs] << 16], top * (1.0 / (FULL * 65536.0))


def unpacked(word):
    return word.astype(jnp.float32), (word << 16).astype(jnp.float32)


def kernel(
    dims,
    live_hbm, rtaper_hbm, staper_hbm, x_hbm, rd_ref, rf_ref, sd_hbm, sf_hbm,
    out_ref,
    live_ref, rtaper_ref, staper_ref, x_ref, sd_ref, sf_ref, in_sem,
    flat, turned, near, near_unit, far, far_unit, halo, sec, got, sum0, sum1, sum2, sum3, acc0, acc1,
    r_d, r_c0, r_c1, r_norm, t_d, t_c0, t_c1,
    halo_send, halo_recv, send_sem, recv_sem,
):
    rows, nt, peers, per_peer, n_rcv, kr, ks = dims
    nb = nt // LANES
    pairs = nb // 2
    chunks = pl.cdiv(per_peer, GROUP)
    me = lax.axis_index("shot")
    side = lax.axis_index("rcv")
    other = 1 - side
    f32 = jnp.float32

    copies = (
        (x_hbm.at[0], x_ref), (live_hbm, live_ref), (rtaper_hbm, rtaper_ref),
        (staper_hbm, staper_ref), (sd_hbm, sd_ref), (sf_hbm, sf_ref),
    )
    loads = [pltpu.make_async_copy(a, b, in_sem.at[n]) for n, (a, b) in enumerate(copies)]
    for load in loads:
        load.start()

    barrier = pltpu.get_barrier_semaphore()

    def greet(i, carry):
        to = lax.rem(me + i, peers)
        pl.semaphore_signal(barrier, inc=1, device_id={"shot": to}, device_id_type=MESH)
        return carry

    pl.semaphore_signal(barrier, inc=1, device_id={"rcv": other}, device_id_type=MESH)
    lax.fori_loop(1, peers, greet, 0)

    for start in (0, EDGE + rows):
        for b in range(pairs + 1):
            near[b, start : start + EDGE, :] = jnp.zeros((EDGE, LANES), jnp.int32)
        near_unit[start : start + EDGE, :] = jnp.zeros((EDGE, LANES), f32)
    flat[...] = jnp.zeros_like(flat)

    lane = lax.broadcasted_iota(jnp.int32, (GROUP, LANES), 1)
    sub = lax.broadcasted_iota(jnp.int32, (GROUP, LANES), 0)

    def spread(column):
        packed = jnp.broadcast_to(column, (GROUP, LANES))
        return packed >> 8, (packed & 255).astype(f32) * (1.0 / 256.0)

    loads[1].wait()
    loads[2].wait()
    live_count = live_ref[0]
    for block in range(rows // LANES):
        cols = slice(block * LANES, (block + 1) * LANES)
        for a in range(kr):
            flat[a : a + 1, :] = rd_ref[a, :, cols] * 256 + rf_ref[a, :, cols]
        turned[block] = jnp.transpose(flat[...], (1, 0))

    def receiver_tables(g, carry):
        at = pl.ds(pl.multiple_of(g * GROUP, GROUP), GROUP)
        columns = turned[g // (LANES // GROUP), pl.ds(pl.multiple_of(lax.rem(g, LANES // GROUP) * GROUP, GROUP), GROUP), :]
        where0 = side * rows + g * GROUP + sub - AR
        fold = jnp.zeros((GROUP, LANES), f32)
        for a in range(kr):
            d, weight = spread(columns[:, a : a + 1])
            where = where0 + a
            live = (where >= 0) & (where < rows * n_rcv) & (where < live_count)
            live = live.astype(f32)
            fold = fold + live
            scale = rtaper_ref[a] * live
            r_d[a, at, :] = d
            r_c0[a, at, :] = scale * (1.0 - weight)
            r_c1[a, at, :] = scale * weight
        r_norm[at, :] = 1.0 / jnp.sqrt(jnp.maximum(fold, 1.0))
        return carry

    lax.fori_loop(0, rows // GROUP, receiver_tables, 0, unroll=4)

    halo_copy = pltpu.make_async_remote_copy(
        src_ref=x_hbm.at[0, pl.ds(pl.multiple_of(other * (rows - EDGE), EDGE), EDGE), :],
        dst_ref=halo,
        send_sem=halo_send,
        recv_sem=halo_recv,
        device_id={"rcv": other},
        device_id_type=MESH,
    )

    def filter_rows(load, base):
        done = [v.astype(f32) for v in smooth([load(b).astype(f32) for b in range(nb)])]
        packed, unit = words(done)
        for b, word in enumerate(packed):
            near[b, pl.ds(base, EDGE), :] = word
        near_unit[pl.ds(base, EDGE), :] = unit

    def filter_own(g, carry):
        start = pl.multiple_of(g * EDGE, EDGE)
        filter_rows(lambda b: x_ref[pl.ds(start, EDGE), b * LANES : (b + 1) * LANES], EDGE + start)
        return carry

    loads[0].wait()
    lax.fori_loop(0, rows // EDGE, filter_own, 0, unroll=4)

    edge_peer = other * (peers - 1)

    half = max(peers // 2, 1)
    mine = me // half
    place = lax.rem(me, half)

    def source(i):
        return half * lax.rem(mine + i // half, peers // half) + lax.rem(place + peers - i, half)

    edge_here = jnp.where(edge_peer // half == mine, 1, 0)
    across = half - 1 + edge_here

    def target(i):
        near_side = jnp.where(i < across, 0, 1)
        step = i - near_side * across
        span = jnp.where(near_side == edge_here, half - 1, half)
        base = jnp.where(near_side == edge_here, side, 0)
        local = base + lax.rem(place + step, jnp.maximum(span, 1))
        block = lax.rem(mine + 1 + near_side, peers // half)
        return jnp.where(i == peers - 1, edge_peer, half * block + local)

    def send_of(to):
        return pltpu.make_async_remote_copy(
            src_ref=sec.at[to],
            dst_ref=got.at[me],
            send_sem=send_sem.at[to],
            recv_sem=recv_sem.at[me],
            device_id={"shot": to},
            device_id_type=MESH,
        )

    def recv_of(origin):
        return pltpu.make_async_remote_copy(
            src_ref=sec.at[origin],
            dst_ref=got.at[origin],
            send_sem=send_sem.at[origin],
            recv_sem=recv_sem.at[origin],
            device_id={"shot": origin},
            device_id_type=MESH,
        )

    def gather(to, sums):
        for c in range(chunks):
            row0 = to * per_peer + c * GROUP
            if per_peer % GROUP == 0:
                row0 = pl.multiple_of(row0, GROUP)
            at = pl.ds(row0, GROUP)
            total0, total1 = [None] * nb, [None] * nb
            for a in range(kr):
                d = r_d[a, at, :]
                source = pl.ds(EDGE - AR + row0 + a, GROUP)
                unit = near_unit[source, :]
                c0, c1 = r_c0[a, at, :] * unit, r_c1[a, at, :] * unit
                idx, own = (lane + d) & (LANES - 1), lane >= d
                now = near[0, source, :]
                for b in range(pairs):
                    after = near[b + 1, source, :]
                    word = jnp.take_along_axis(jnp.where(own, now, after), idx, axis=1)
                    now = after
                    for n, value in zip((b, b + pairs), unpacked(word)):
                        total0[n] = c0 * value if a == 0 else total0[n] + c0 * value
                        total1[n] = c1 * value if a == 0 else total1[n] + c1 * value
            norm = r_norm[at, :]
            rows_of = slice(c * GROUP, c * GROUP + GROUP)
            for b in range(nb):
                sums[0][b, rows_of, :] = total0[b] * norm
                sums[1][b, rows_of, :] = total1[b] * norm

    def emit(to, sums):
        later = ahead([sums[1][b].astype(jnp.bfloat16).astype(f32) for b in range(nb)])
        one = [(sums[0][b] + later[b]).astype(jnp.bfloat16).astype(f32) for b in range(nb)]
        for b, value in enumerate(smooth(one)):
            sec[to, :, b * LANES : (b + 1) * LANES] = value[:per_peer]


    def dispatch(to):
        @pl.when(to != me)
        def _():
            send_of(to).start()

        @pl.when(to == me)
        def _():
            got[me] = sec[me]

    even, odd = (sum0, sum1), (sum2, sum3)
    gather(target(0), even)
    emit(target(0), even)
    pl.semaphore_wait(barrier, peers)
    halo_copy.start()
    dispatch(target(0))
    if peers > 1:
        gather(target(1), odd)

        def receiver_steps(n, carry):
            for i, now, then in ((2 * n + 1, odd, even), (2 * n + 2, even, odd)):
                @pl.when(i == peers - 2)
                def _():
                    halo_copy.wait_recv()
                    filter_rows(
                        lambda b: halo[:, b * LANES : (b + 1) * LANES],
                        pl.multiple_of(other * (EDGE + rows), EDGE),
                    )

                gather(target(i + 1), then)
                emit(target(i), now)
                dispatch(target(i))
            return carry

        lax.fori_loop(0, peers // 2 - 1, receiver_steps, 0)
        emit(target(peers - 1), odd)
        dispatch(target(peers - 1))

    for n in (3, 4, 5):
        loads[n].wait()
    group = LANES // EDGE

    def source_tables(g, carry):
        for kk in range(group):
            for a in range(ks):
                at = kk * EDGE + a
                flat[at : at + 1, :per_peer] = sd_ref[g * group + kk, a] * 256 + sf_ref[g * group + kk, a]
        turned[0] = jnp.transpose(flat[...], (1, 0))
        for kk in range(group):
            k = g * group + kk
            count = jnp.minimum(k + ks - AS, peers) - jnp.maximum(k - AS, 0)
            norm = 1.0 / jnp.sqrt(jnp.full((GROUP, LANES), count, jnp.int32).astype(f32))
            for c in range(chunks):
                at = slice(c * GROUP, c * GROUP + GROUP)
                columns = turned[0, at, :]
                for a in range(ks):
                    d, weight = spread(columns[:, kk * EDGE + a : kk * EDGE + a + 1])
                    scale = staper_ref[a] * norm
                    t_d[k, a, at, :] = d
                    t_c0[k, a, at, :] = scale * (1.0 - weight)
                    t_c1[k, a, at, :] = scale * weight
        return carry

    lax.fori_loop(0, peers // group, source_tables, 0)

    def clear(k, carry):
        for b in range(nb):
            acc0[k, b] = jnp.zeros(acc0.shape[2:], f32)
            acc1[k, b] = jnp.zeros(acc1.shape[2:], f32)
        return carry

    lax.fori_loop(0, peers, clear, 0)

    if per_peer < GROUP:
        for b in range(pairs + 1):
            far[b] = jnp.zeros(far.shape[1:], jnp.int32)
        far_unit[...] = jnp.zeros(far_unit.shape, f32)
    width = min(peers, ks)

    def shot_sum(p, block_of):
        packed, unit = words([block_of(b).astype(f32) for b in range(nb)])
        for b, word in enumerate(packed):
            far[b, :per_peer, :] = word
        far_unit[:per_peer, :] = unit
        base = 0 if width == peers else jnp.minimum(jnp.maximum(p - AS, 0), peers - width)
        for kk in range(width):
            k = base + kk
            tap = p - k + AS
            a = jnp.minimum(jnp.maximum(tap, 0), ks - 1)
            inside = jnp.where(tap == a, 1.0, 0.0)
            for c in range(chunks):
                at = slice(c * GROUP, c * GROUP + GROUP)
                d, unit = t_d[k, a, at, :], far_unit[at, :] * inside
                c0, c1 = t_c0[k, a, at, :] * unit, t_c1[k, a, at, :] * unit
                idx, own = (lane + d) & (LANES - 1), lane >= d
                now = far[0, at, :]
                for b in range(pairs):
                    after = far[b + 1, at, :]
                    word = jnp.take_along_axis(jnp.where(own, now, after), idx, axis=1)
                    now = after
                    for n, value in zip((b, b + pairs), unpacked(word)):
                        acc0[k, n, at, :] += c0 * value
                        acc1[k, n, at, :] += c1 * value

    def source_step(i, carry):
        origin = source(i)

        @pl.when(i > 0)
        def _():
            recv_of(origin).wait_recv()

        shot_sum(origin, lambda b: got[origin, :, b * LANES : (b + 1) * LANES])
        return carry

    lax.fori_loop(0, peers, source_step, 0)

    def finish(k, carry):
        later = ahead([acc1[k, b].astype(jnp.bfloat16).astype(f32) for b in range(nb)])
        for b in range(nb):
            value = (acc0[k, b] + later[b]).astype(jnp.bfloat16)
            out_ref[k, 0, :, b * LANES : (b + 1) * LANES] = value[:per_peer]
        return carry

    lax.fori_loop(0, peers, finish, 0, unroll=4)

    halo_copy.wait_send()

    def drain(i, carry):
        send_of(source(i)).wait_send()
        return carry

    lax.fori_loop(1, peers, drain, 0)


def body(traces, rcv_delay, rcv_frac, live_count, src_delay, src_frac, rcv_taper, src_taper):
    _, rows, nt = traces.shape
    peers = lax.axis_size("shot")
    n_rcv = lax.axis_size("rcv")
    per_peer = rows // peers
    kr, ks = rcv_delay.shape[-1], src_delay.shape[-1]
    nb = nt // LANES
    tall = pl.cdiv(per_peer, GROUP) * GROUP
    rcv_delay, rcv_frac = (jnp.transpose(v, (2, 0, 1)) for v in (rcv_delay, rcv_frac))
    src_delay, src_frac = (jnp.transpose(v, (0, 3, 1, 2)) for v in (src_delay, src_frac))
    dims = (rows, nt, peers, per_peer, n_rcv, kr, ks)
    hbm, vmem = pl.BlockSpec(memory_space=pltpu.HBM), pl.BlockSpec(memory_space=pltpu.VMEM)
    keep = functools.partial(pltpu.with_memory_space_constraint, memory_space=pltpu.HBM)
    near = functools.partial(pltpu.with_memory_space_constraint, memory_space=pltpu.VMEM)
    f32, bf16, i32 = jnp.float32, jnp.bfloat16, jnp.int32
    extended = (nb // 2 + 1, rows + 2 * EDGE, LANES)
    r_table = (kr, rows + GROUP, LANES)
    t_table = (peers, ks, tall, LANES)
    return pl.pallas_call(
        functools.partial(kernel, dims),
        name="redatum",
        out_shape=pltpu.VMEM((peers, 1, per_peer, nt), bf16),
        in_specs=[hbm] * 4 + [vmem] * 2 + [hbm] * 2,
        out_specs=pl.BlockSpec(memory_space=pltpu.VMEM),
        scratch_shapes=[
            pltpu.SMEM((1,), i32),
            pltpu.SMEM((kr,), f32),
            pltpu.SMEM((ks,), f32),
            pltpu.VMEM((rows, nt), bf16),
            pltpu.VMEM(src_delay.shape, i32),
            pltpu.VMEM(src_delay.shape, i32),
            pltpu.SemaphoreType.DMA((6,)),
            pltpu.VMEM((LANES, LANES), i32),
            pltpu.VMEM((rows // LANES, LANES, LANES), i32),
            pltpu.VMEM(extended, i32),
            pltpu.VMEM(extended[1:], f32),
            pltpu.VMEM((nb // 2 + 1, tall, LANES), i32),
            pltpu.VMEM((tall, LANES), f32),
            pltpu.VMEM((EDGE, nt), bf16),
            pltpu.VMEM((peers, per_peer, nt), bf16),
            pltpu.VMEM((peers, per_peer, nt), bf16),
            pltpu.VMEM((nb, tall, LANES), f32),
            pltpu.VMEM((nb, tall, LANES), f32),
            pltpu.VMEM((nb, tall, LANES), f32),
            pltpu.VMEM((nb, tall, LANES), f32),
            pltpu.VMEM((peers, nb, tall, LANES), f32),
            pltpu.VMEM((peers, nb, tall, LANES), f32),
            pltpu.VMEM(r_table, i32),
            pltpu.VMEM(r_table, f32),
            pltpu.VMEM(r_table, f32),
            pltpu.VMEM(r_table[1:], f32),
            pltpu.VMEM(t_table, i32),
            pltpu.VMEM(t_table, f32),
            pltpu.VMEM(t_table, f32),
            pltpu.SemaphoreType.DMA,
            pltpu.SemaphoreType.DMA,
            pltpu.SemaphoreType.DMA((peers,)),
            pltpu.SemaphoreType.DMA((peers,)),
        ],
        compiler_params=pltpu.CompilerParams(
            collective_id=0, has_side_effects=True, vmem_limit_bytes=60 * 2**20
        ),
    )(
        live_count, keep(rcv_taper), keep(src_taper), keep(traces), near(rcv_delay), near(rcv_frac), keep(src_delay), keep(src_frac)
    )


def solution(mesh):
    return jax.shard_map(
        body,
        mesh=mesh,
        in_specs=(
            P(("slab", "shot"), "rcv", None),
            P(("slab", "shot"), "rcv", None),
            P(("slab", "shot"), "rcv", None),
            P(("slab", "shot")),
            P("slab", "rcv", "shot", None),
            P("slab", "rcv", "shot", None),
            P(),
            P(),
        ),
        out_specs=P("slab", "rcv", "shot", None),
        check_vma=False,
    )
```

```python
import functools

import jax
import jax.numpy as jnp
import numpy as np
from jax import lax
from jax.experimental import pallas as pl
from jax.experimental.pallas import tpu as pltpu
from jax.sharding import PartitionSpec as P

AR = 4
AS = 4
TRI = 2
LANES = 128
GROUP = 8
EDGE = 16
FULL = 32000.0
TINY = 1e-30
MESH = pl.DeviceIdType.MESH


def taps_of_filter():
    heights = np.maximum(TRI - np.abs(np.arange(-TRI, TRI + 1)), 0).astype(np.float32)
    taps = (heights / np.sqrt(np.sum(heights**2, dtype=np.float32))).astype(jnp.bfloat16)
    return [float(v) for v in taps[TRI:]]


MAIN_TAP, SIDE_TAP = taps_of_filter()[:2]


def ends(shape):
    lane = lax.broadcasted_iota(jnp.int32, shape, 1)
    return lane == 0, lane == LANES - 1


def smooth(raw):
    is_first, is_last = ends(raw[0].shape)
    zero = jnp.zeros_like(raw[0])
    up = [zero] + [pltpu.roll(x, 1, 1) for x in raw]
    down = [pltpu.roll(x, LANES - 1, 1) for x in raw] + [zero]
    done = []
    for b, x in enumerate(raw):
        before = jnp.where(is_first, up[b], up[b + 1])
        after = jnp.where(is_last, down[b + 1], down[b])
        done.append((MAIN_TAP * x + SIDE_TAP * (before + after)).astype(jnp.bfloat16))
    return done


def ahead(values):
    _, is_last = ends(values[0].shape)
    rolled = [pltpu.roll(x, LANES - 1, 1) for x in values] + [jnp.zeros_like(values[0])]
    return [jnp.where(is_last, rolled[b + 1], rolled[b]) for b in range(len(values))]


def words(values):
    pairs = len(values) // 2
    top = functools.reduce(jnp.maximum, [jnp.abs(v) for v in values])
    top = jnp.maximum(jnp.max(top, axis=1, keepdims=True), TINY)
    top = jnp.broadcast_to(top, values[0].shape)
    scale = FULL / top
    whole = [(v * scale).astype(jnp.int32) for v in values]
    packed = [(whole[b] << 16) + whole[b + pairs] for b in range(pairs)]
    return packed + [whole[pairs] << 16], top * (1.0 / (FULL * 65536.0))


def unpacked(word):
    return word.astype(jnp.float32), (word << 16).astype(jnp.float32)


def kernel(
    dims,
    live_hbm, rtaper_hbm, staper_hbm, x_hbm, rd_ref, rf_ref, sd_hbm, sf_hbm,
    out_ref,
    live_ref, rtaper_ref, staper_ref, x_ref, sd_ref, sf_ref, in_sem,
    flat, turned, near, near_unit, far, far_unit, far1, far1_unit, halo, sec, got, sum0, sum1, sum2, sum3, acc0, acc1,
    r_d, r_w, t_d, t_c0, t_c1,
    halo_send, halo_recv, send_sem, recv_sem,
):
    rows, nt, peers, per_peer, n_rcv, kr, ks = dims
    nb = nt // LANES
    pairs = nb // 2
    chunks = pl.cdiv(per_peer, GROUP)
    me = lax.axis_index("shot")
    side = lax.axis_index("rcv")
    other = 1 - side
    f32 = jnp.float32

    copies = (
        (x_hbm.at[0], x_ref), (live_hbm, live_ref), (rtaper_hbm, rtaper_ref),
        (staper_hbm, staper_ref), (sd_hbm, sd_ref), (sf_hbm, sf_ref),
    )
    loads = [pltpu.make_async_copy(a, b, in_sem.at[n]) for n, (a, b) in enumerate(copies)]
    for load in loads:
        load.start()

    barrier = pltpu.get_barrier_semaphore()

    def greet(i, carry):
        to = lax.rem(me + i, peers)
        pl.semaphore_signal(barrier, inc=1, device_id={"shot": to}, device_id_type=MESH)
        return carry

    @pl.when(side == 0)
    def _():
        pl.semaphore_signal(barrier, inc=1, device_id={"rcv": other}, device_id_type=MESH)

    lax.fori_loop(1, peers, greet, 0)

    for start in (0, EDGE + rows):
        for b in range(pairs + 1):
            near[b, start : start + EDGE, :] = jnp.zeros((EDGE, LANES), jnp.int32)
        near_unit[start : start + EDGE, :] = jnp.zeros((EDGE, LANES), f32)
    flat[...] = jnp.zeros_like(flat)

    lane = lax.broadcasted_iota(jnp.int32, (GROUP, LANES), 1)
    sub = lax.broadcasted_iota(jnp.int32, (GROUP, LANES), 0)

    def spread(column):
        packed = jnp.broadcast_to(column, (GROUP, LANES))
        return packed >> 8, (packed & 255).astype(f32) * (1.0 / 256.0)

    for block in range(rows // LANES):
        cols = slice(block * LANES, (block + 1) * LANES)
        for a in range(kr):
            flat[a : a + 1, :] = rd_ref[a, :, cols] * 256 + rf_ref[a, :, cols]
        turned[block] = jnp.transpose(flat[...], (1, 0))

    def receiver_tables(g, carry):
        at = pl.ds(pl.multiple_of(g * GROUP, GROUP), GROUP)
        columns = turned[g // (LANES // GROUP), pl.ds(pl.multiple_of(lax.rem(g, LANES // GROUP) * GROUP, GROUP), GROUP), :]
        for a in range(kr):
            d, weight = spread(columns[:, a : a + 1])
            r_d[a, at, :] = d
            r_w[a, at, :] = weight
        return carry

    lax.fori_loop(0, rows // GROUP, receiver_tables, 0, unroll=4)

    halo_copy = pltpu.make_async_remote_copy(
        src_ref=x_hbm.at[0, pl.ds(pl.multiple_of(other * (rows - EDGE), EDGE), EDGE), :],
        dst_ref=halo,
        send_sem=halo_send,
        recv_sem=halo_recv,
        device_id={"rcv": other},
        device_id_type=MESH,
    )

    def filter_rows(load, base):
        done = [v.astype(f32) for v in smooth([load(b).astype(f32) for b in range(nb)])]
        packed, unit = words(done)
        where = side * rows + base - EDGE + lax.broadcasted_iota(jnp.int32, (EDGE, LANES), 0)
        unit = jnp.where(where < live_count, unit, 0.0)
        for b, word in enumerate(packed):
            near[b, pl.ds(base, EDGE), :] = word
        near_unit[pl.ds(base, EDGE), :] = unit

    def filter_own(g, carry):
        start = pl.multiple_of(g * EDGE, EDGE)
        filter_rows(lambda b: x_ref[pl.ds(start, EDGE), b * LANES : (b + 1) * LANES], EDGE + start)
        return carry

    for n in range(3):
        loads[n].wait()
    live_count = live_ref[0]

    edge_peer = other * (peers - 1)

    half = max(peers // 2, 1)

    def across(m):
        total, unit = 0, 1
        while unit < peers:
            x, y = lax.rem(me // unit, 2), lax.rem(m // unit, 2)
            total = total + unit * (x + y - 2 * x * y)
            unit *= 2
        return total

    def partner(m, i):
        return across(m) if peers & (peers - 1) == 0 else lax.rem(me + i, peers)

    def source(i):
        far_half = half + (i - half) + 1 - 2 * lax.rem(i, 2)
        return partner(jnp.where(i == 0, 0, jnp.where(i < half, half - i, far_half)), i)

    def rank(i):
        return partner(jnp.where(i < half, half + i + 1 - 2 * lax.rem(i, 2), peers - 1 - i), i + 1)

    def place_of(to):
        if peers & (peers - 1):
            return lax.rem(to - me - 1 + 2 * peers, peers)
        m = across(to)
        return jnp.where(m < half, peers - 1 - m, m - half + 1 - 2 * lax.rem(m, 2))

    edge_place = place_of(edge_peer)

    def target(i):
        skipped = jnp.where(i >= edge_place, i + 1, i)
        return rank(jnp.where(i == peers - 1, edge_place, skipped))

    def send_of(to):
        return pltpu.make_async_remote_copy(
            src_ref=sec.at[to],
            dst_ref=got.at[me],
            send_sem=send_sem.at[to],
            recv_sem=recv_sem.at[me],
            device_id={"shot": to},
            device_id_type=MESH,
        )

    def recv_of(origin):
        return pltpu.make_async_remote_copy(
            src_ref=sec.at[origin],
            dst_ref=got.at[origin],
            send_sem=send_sem.at[origin],
            recv_sem=recv_sem.at[origin],
            device_id={"shot": origin},
            device_id_type=MESH,
        )

    def gather(to, sums):
        for c in range(chunks):
            row0 = to * per_peer + c * GROUP
            if per_peer % GROUP == 0:
                row0 = pl.multiple_of(row0, GROUP)
            at = pl.ds(row0, GROUP)
            total0, total1 = [None] * nb, [None] * nb
            for a in range(kr):
                d = r_d[a, at, :]
                source = pl.ds(EDGE - AR + row0 + a, GROUP)
                unit = near_unit[source, :]
                whole = rtaper_ref[a] * unit
                c1 = whole * r_w[a, at, :]
                c0 = whole - c1
                idx, own = (lane + d) & (LANES - 1), lane >= d
                now = near[0, source, :]
                for b in range(pairs):
                    after = near[b + 1, source, :]
                    word = jnp.take_along_axis(jnp.where(own, now, after), idx, axis=1)
                    now = after
                    for n, value in zip((b, b + pairs), unpacked(word)):
                        total0[n] = c0 * value if a == 0 else total0[n] + c0 * value
                        total1[n] = c1 * value if a == 0 else total1[n] + c1 * value
            where = side * rows + row0 + sub
            last = jnp.minimum(jnp.minimum(live_count, rows * n_rcv) - 1, where + AR)
            fold = last - jnp.maximum(where - AR, 0) + 1
            norm = 1.0 / jnp.sqrt(jnp.maximum(fold, 1).astype(f32))
            rows_of = slice(c * GROUP, c * GROUP + GROUP)
            for b in range(nb):
                sums[0][b, rows_of, :] = total0[b] * norm
                sums[1][b, rows_of, :] = total1[b] * norm

    def emit(to, sums):
        later = ahead([sums[1][b].astype(jnp.bfloat16).astype(f32) for b in range(nb)])
        one = [(sums[0][b] + later[b]).astype(jnp.bfloat16).astype(f32) for b in range(nb)]
        for b, value in enumerate(smooth(one)):
            sec[to, :, b * LANES : (b + 1) * LANES] = value[:per_peer]


    def dispatch(to):
        @pl.when(to != me)
        def _():
            send_of(to).start()

        @pl.when(to == me)
        def _():
            got[me] = sec[me]

    even, odd = (sum0, sum1), (sum2, sum3)
    def filter_all():
        lax.fori_loop(0, rows // EDGE, filter_own, 0, unroll=4)

    if per_peer == EDGE:
        for step in (-1, 0, 1):
            filter_own(jnp.minimum(jnp.maximum(target(0) + step, 0), peers - 1), 0)
    else:
        filter_all()
    gather(target(0), even)
    emit(target(0), even)
    pl.semaphore_wait(barrier, peers - 1 + side)

    @pl.when(side == 1)
    def _():
        halo_copy.start()

    dispatch(target(0))
    if per_peer == EDGE:
        filter_all()
    if peers > 1:
        gather(target(1), odd)

        def receiver_steps(n, carry):
            for i, now, then in ((2 * n + 1, odd, even), (2 * n + 2, even, odd)):
                @pl.when(i == peers - 2)
                def _():
                    halo_copy.wait_recv()

                    @pl.when(side == 0)
                    def _():
                        halo_copy.start()

                    filter_rows(
                        lambda b: halo[:, b * LANES : (b + 1) * LANES],
                        pl.multiple_of(other * (EDGE + rows), EDGE),
                    )

                gather(target(i + 1), then)
                emit(target(i), now)
                dispatch(target(i))
            return carry

        lax.fori_loop(0, peers // 2 - 1, receiver_steps, 0)
        emit(target(peers - 1), odd)
        dispatch(target(peers - 1))

    for n in (3, 4, 5):
        loads[n].wait()
    group = LANES // EDGE

    def source_tables(g, carry):
        for kk in range(group):
            for a in range(ks):
                at = kk * EDGE + a
                flat[at : at + 1, :per_peer] = sd_ref[g * group + kk, a] * 256 + sf_ref[g * group + kk, a]
        turned[0] = jnp.transpose(flat[...], (1, 0))
        for kk in range(group):
            k = g * group + kk
            count = jnp.minimum(k + ks - AS, peers) - jnp.maximum(k - AS, 0)
            norm = 1.0 / jnp.sqrt(jnp.full((GROUP, LANES), count, jnp.int32).astype(f32))
            for c in range(chunks):
                at = slice(c * GROUP, c * GROUP + GROUP)
                columns = turned[0, at, :]
                for a in range(ks):
                    d, weight = spread(columns[:, kk * EDGE + a : kk * EDGE + a + 1])
                    scale = staper_ref[a] * norm
                    t_d[k, a, at, :] = d
                    t_c0[k, a, at, :] = scale * (1.0 - weight)
                    t_c1[k, a, at, :] = scale * weight
        return carry

    lax.fori_loop(0, peers // group, source_tables, 0)

    def clear(k, carry):
        for b in range(nb):
            acc0[k, b] = jnp.zeros(acc0.shape[2:], f32)
            acc1[k, b] = jnp.zeros(acc1.shape[2:], f32)
        return carry

    lax.fori_loop(0, peers, clear, 0)

    if per_peer < GROUP:
        for table in ((far, far_unit), (far1, far1_unit)):
            table[0][...] = jnp.zeros(far.shape, jnp.int32)
            table[1][...] = jnp.zeros(far_unit.shape, f32)
    width = min(peers, ks)

    def prepare(p, table):
        packed, unit = words([got[p, :, b * LANES : (b + 1) * LANES].astype(f32) for b in range(nb)])
        for b, word in enumerate(packed):
            table[0][b, :per_peer, :] = word
        table[1][:per_peer, :] = unit

    def accumulate(p, table):
        base = 0 if width == peers else jnp.minimum(jnp.maximum(p - AS, 0), peers - width)
        for kk in range(width):
            k = base + kk
            tap = p - k + AS
            a = jnp.minimum(jnp.maximum(tap, 0), ks - 1)
            inside = jnp.where(tap == a, 1.0, 0.0)
            for c in range(chunks):
                at = slice(c * GROUP, c * GROUP + GROUP)
                d, unit = t_d[k, a, at, :], table[1][at, :] * inside
                c0, c1 = t_c0[k, a, at, :] * unit, t_c1[k, a, at, :] * unit
                idx, own = (lane + d) & (LANES - 1), lane >= d
                now = table[0][0, at, :]
                for b in range(pairs):
                    after = table[0][b + 1, at, :]
                    word = jnp.take_along_axis(jnp.where(own, now, after), idx, axis=1)
                    now = after
                    for n, value in zip((b, b + pairs), unpacked(word)):
                        acc0[k, n, at, :] += c0 * value
                        acc1[k, n, at, :] += c1 * value

    def arrive(i, table):
        recv_of(source(i)).wait_recv()
        prepare(source(i), table)

    first, second = (far, far_unit), (far1, far1_unit)
    prepare(me, first)

    def source_steps(n, carry):
        arrive(2 * n + 1, second)
        accumulate(source(2 * n), first)
        arrive(2 * n + 2, first)
        accumulate(source(2 * n + 1), second)
        return carry

    if peers > 1:
        lax.fori_loop(0, peers // 2 - 1, source_steps, 0)
        arrive(peers - 1, second)
        accumulate(source(peers - 2), first)
        accumulate(source(peers - 1), second)
    else:
        accumulate(me, first)

    def finish(k, carry):
        later = ahead([acc1[k, b].astype(jnp.bfloat16).astype(f32) for b in range(nb)])
        for b in range(nb):
            value = (acc0[k, b] + later[b]).astype(jnp.bfloat16)
            out_ref[k, 0, :, b * LANES : (b + 1) * LANES] = value[:per_peer]
        return carry

    lax.fori_loop(0, peers, finish, 0, unroll=min(peers, 8))

    halo_copy.wait_send()

    def drain(i, carry):
        send_of(source(i)).wait_send()
        return carry

    lax.fori_loop(1, peers, drain, 0)


def body(traces, rcv_delay, rcv_frac, live_count, src_delay, src_frac, rcv_taper, src_taper):
    _, rows, nt = traces.shape
    peers = lax.axis_size("shot")
    n_rcv = lax.axis_size("rcv")
    per_peer = rows // peers
    kr, ks = rcv_delay.shape[-1], src_delay.shape[-1]
    nb = nt // LANES
    tall = pl.cdiv(per_peer, GROUP) * GROUP
    rcv_delay, rcv_frac = (jnp.transpose(v, (2, 0, 1)) for v in (rcv_delay, rcv_frac))
    src_delay, src_frac = (jnp.transpose(v, (0, 3, 1, 2)) for v in (src_delay, src_frac))
    dims = (rows, nt, peers, per_peer, n_rcv, kr, ks)
    hbm, vmem = pl.BlockSpec(memory_space=pltpu.HBM), pl.BlockSpec(memory_space=pltpu.VMEM)
    keep = functools.partial(pltpu.with_memory_space_constraint, memory_space=pltpu.HBM)
    near = functools.partial(pltpu.with_memory_space_constraint, memory_space=pltpu.VMEM)
    f32, bf16, i32 = jnp.float32, jnp.bfloat16, jnp.int32
    extended = (nb // 2 + 1, rows + 2 * EDGE, LANES)
    r_table = (kr, rows + GROUP, LANES)
    t_table = (peers, ks, tall, LANES)
    return pl.pallas_call(
        functools.partial(kernel, dims),
        name="redatum",
        out_shape=pltpu.VMEM((peers, 1, per_peer, nt), bf16),
        in_specs=[hbm] * 4 + [vmem] * 2 + [hbm] * 2,
        out_specs=pl.BlockSpec(memory_space=pltpu.VMEM),
        scratch_shapes=[
            pltpu.SMEM((1,), i32),
            pltpu.SMEM((kr,), f32),
            pltpu.SMEM((ks,), f32),
            pltpu.VMEM((rows, nt), bf16),
            pltpu.VMEM(src_delay.shape, i32),
            pltpu.VMEM(src_delay.shape, i32),
            pltpu.SemaphoreType.DMA((6,)),
            pltpu.VMEM((LANES, LANES), i32),
            pltpu.VMEM((rows // LANES, LANES, LANES), i32),
            pltpu.VMEM(extended, i32),
            pltpu.VMEM(extended[1:], f32),
            pltpu.VMEM((nb // 2 + 1, tall, LANES), i32),
            pltpu.VMEM((tall, LANES), f32),
            pltpu.VMEM((nb // 2 + 1, tall, LANES), i32),
            pltpu.VMEM((tall, LANES), f32),
            pltpu.VMEM((EDGE, nt), bf16),
            pltpu.VMEM((peers, per_peer, nt), bf16),
            pltpu.VMEM((peers, per_peer, nt), bf16),
            pltpu.VMEM((nb, tall, LANES), f32),
            pltpu.VMEM((nb, tall, LANES), f32),
            pltpu.VMEM((nb, tall, LANES), f32),
            pltpu.VMEM((nb, tall, LANES), f32),
            pltpu.VMEM((peers, nb, tall, LANES), f32),
            pltpu.VMEM((peers, nb, tall, LANES), f32),
            pltpu.VMEM(r_table, i32),
            pltpu.VMEM(r_table, f32),
            pltpu.VMEM(t_table, i32),
            pltpu.VMEM(t_table, f32),
            pltpu.VMEM(t_table, f32),
            pltpu.SemaphoreType.DMA,
            pltpu.SemaphoreType.DMA,
            pltpu.SemaphoreType.DMA((peers,)),
            pltpu.SemaphoreType.DMA((peers,)),
        ],
        compiler_params=pltpu.CompilerParams(
            collective_id=0, has_side_effects=True, vmem_limit_bytes=60 * 2**20
        ),
    )(
        live_count, keep(rcv_taper), keep(src_taper), keep(traces), near(rcv_delay), near(rcv_frac), keep(src_delay), keep(src_frac)
    )


def solution(mesh):
    return jax.shard_map(
        body,
        mesh=mesh,
        in_specs=(
            P(("slab", "shot"), "rcv", None),
            P(("slab", "shot"), "rcv", None),
            P(("slab", "shot"), "rcv", None),
            P(("slab", "shot")),
            P("slab", "rcv", "shot", None),
            P("slab", "rcv", "shot", None),
            P(),
            P(),
        ),
        out_specs=P("slab", "rcv", "shot", None),
        check_vma=False,
    )
```

```python
import functools

import jax
import jax.numpy as jnp
import numpy as np
from jax import lax
from jax.experimental import pallas as pl
from jax.experimental.pallas import tpu as pltpu
from jax.sharding import PartitionSpec as P

AR = 4
AS = 4
TRI = 2
LANES = 128
GROUP = 8
EDGE = 16
FULL = 32000.0
TINY = 1e-30
MESH = pl.DeviceIdType.MESH


def taps_of_filter():
    heights = np.maximum(TRI - np.abs(np.arange(-TRI, TRI + 1)), 0).astype(np.float32)
    taps = (heights / np.sqrt(np.sum(heights**2, dtype=np.float32))).astype(jnp.bfloat16)
    return [float(v) for v in taps[TRI:]]


MAIN_TAP, SIDE_TAP = taps_of_filter()[:2]


def ends(shape):
    lane = lax.broadcasted_iota(jnp.int32, shape, 1)
    return lane == 0, lane == LANES - 1


def smooth(raw):
    is_first, is_last = ends(raw[0].shape)
    zero = jnp.zeros_like(raw[0])
    up = [zero] + [pltpu.roll(x, 1, 1) for x in raw]
    down = [pltpu.roll(x, LANES - 1, 1) for x in raw] + [zero]
    done = []
    for b, x in enumerate(raw):
        before = jnp.where(is_first, up[b], up[b + 1])
        after = jnp.where(is_last, down[b + 1], down[b])
        done.append((MAIN_TAP * x + SIDE_TAP * (before + after)).astype(jnp.bfloat16))
    return done


def ahead(values):
    _, is_last = ends(values[0].shape)
    rolled = [pltpu.roll(x, LANES - 1, 1) for x in values] + [jnp.zeros_like(values[0])]
    return [jnp.where(is_last, rolled[b + 1], rolled[b]) for b in range(len(values))]


def words(values):
    pairs = len(values) // 2
    top = functools.reduce(jnp.maximum, [jnp.abs(v) for v in values])
    top = jnp.maximum(jnp.max(top, axis=1, keepdims=True), TINY)
    top = jnp.broadcast_to(top, values[0].shape)
    scale = FULL / top
    whole = [(v * scale).astype(jnp.int32) for v in values]
    packed = [(whole[b] << 16) + whole[b + pairs] for b in range(pairs)]
    return packed + [whole[pairs] << 16], top * (1.0 / (FULL * 65536.0))


def unpacked(word):
    return word.astype(jnp.float32), (word << 16).astype(jnp.float32)


def kernel(
    dims,
    live_hbm, rtaper_hbm, staper_hbm, x_hbm, rd_ref, rf_ref, sd_hbm, sf_hbm,
    out_ref,
    live_ref, rtaper_ref, staper_ref, x_ref, sd_ref, sf_ref, in_sem,
    flat, turned, near, near_unit, far, far_unit, far1, far1_unit, halo, sec, got, sum0, sum1, sum2, sum3, acc0, acc1,
    r_d, r_w, t_d, t_c0, t_c1,
    halo_send, halo_recv, send_sem, recv_sem,
):
    rows, nt, peers, per_peer, n_rcv, kr, ks = dims
    nb = nt // LANES
    pairs = nb // 2
    chunks = pl.cdiv(per_peer, GROUP)
    me = lax.axis_index("shot")
    side = lax.axis_index("rcv")
    other = 1 - side
    f32 = jnp.float32

    copies = (
        (x_hbm.at[0], x_ref), (live_hbm, live_ref), (rtaper_hbm, rtaper_ref),
        (staper_hbm, staper_ref), (sd_hbm, sd_ref), (sf_hbm, sf_ref),
    )
    loads = [pltpu.make_async_copy(a, b, in_sem.at[n]) for n, (a, b) in enumerate(copies)]
    for load in loads:
        load.start()

    barrier = pltpu.get_barrier_semaphore()

    def greet(i, carry):
        to = lax.rem(me + i, peers)
        pl.semaphore_signal(barrier, inc=1, device_id={"shot": to}, device_id_type=MESH)
        return carry

    @pl.when(side == 0)
    def _():
        pl.semaphore_signal(barrier, inc=1, device_id={"rcv": other}, device_id_type=MESH)

    lax.fori_loop(1, peers, greet, 0)

    for start in (0, EDGE + rows):
        for b in range(pairs + 1):
            near[b, start : start + EDGE, :] = jnp.zeros((EDGE, LANES), jnp.int32)
        near_unit[start : start + EDGE, :] = jnp.zeros((EDGE, LANES), f32)
    flat[...] = jnp.zeros_like(flat)

    lane = lax.broadcasted_iota(jnp.int32, (GROUP, LANES), 1)
    sub = lax.broadcasted_iota(jnp.int32, (GROUP, LANES), 0)

    def spread(column):
        packed = jnp.broadcast_to(column, (GROUP, LANES))
        return packed >> 8, (packed & 255).astype(f32) * (1.0 / 256.0)

    for block in range(rows // LANES):
        cols = slice(block * LANES, (block + 1) * LANES)
        for a in range(kr):
            flat[a : a + 1, :] = rd_ref[a, :, cols] * 256 + rf_ref[a, :, cols]
        turned[block] = jnp.transpose(flat[...], (1, 0))

    def receiver_tables(g, carry):
        at = pl.ds(pl.multiple_of(g * GROUP, GROUP), GROUP)
        columns = turned[g // (LANES // GROUP), pl.ds(pl.multiple_of(lax.rem(g, LANES // GROUP) * GROUP, GROUP), GROUP), :]
        for a in range(kr):
            d, weight = spread(columns[:, a : a + 1])
            r_d[a, at, :] = d
            r_w[a, at, :] = weight
        return carry

    lax.fori_loop(0, rows // GROUP, receiver_tables, 0, unroll=4)

    halo_copy = pltpu.make_async_remote_copy(
        src_ref=x_hbm.at[0, pl.ds(pl.multiple_of(other * (rows - EDGE), EDGE), EDGE), :],
        dst_ref=halo,
        send_sem=halo_send,
        recv_sem=halo_recv,
        device_id={"rcv": other},
        device_id_type=MESH,
    )

    def filter_rows(load, base):
        done = [v.astype(f32) for v in smooth([load(b).astype(f32) for b in range(nb)])]
        packed, unit = words(done)
        where = side * rows + base - EDGE + lax.broadcasted_iota(jnp.int32, (EDGE, LANES), 0)
        unit = jnp.where(where < live_count, unit, 0.0)
        for b, word in enumerate(packed):
            near[b, pl.ds(base, EDGE), :] = word
        near_unit[pl.ds(base, EDGE), :] = unit

    def filter_own(g, carry):
        start = pl.multiple_of(g * EDGE, EDGE)
        filter_rows(lambda b: x_ref[pl.ds(start, EDGE), b * LANES : (b + 1) * LANES], EDGE + start)
        return carry

    for n in range(3):
        loads[n].wait()
    live_count = live_ref[0]

    edge_peer = other * (peers - 1)

    half = max(peers // 2, 1)

    def across(m):
        total, unit = 0, 1
        while unit < peers:
            x, y = lax.rem(me // unit, 2), lax.rem(m // unit, 2)
            total = total + unit * (x + y - 2 * x * y)
            unit *= 2
        return total

    def partner(m, i):
        return across(m) if peers & (peers - 1) == 0 else lax.rem(me + i, peers)

    def source(i):
        far_half = half + (i - half) + 1 - 2 * lax.rem(i, 2)
        return partner(jnp.where(i == 0, 0, jnp.where(i < half, half - i, far_half)), i)

    def rank(i):
        return partner(jnp.where(i < half, half + i + 1 - 2 * lax.rem(i, 2), peers - 1 - i), i + 1)

    def place_of(to):
        if peers & (peers - 1):
            return lax.rem(to - me - 1 + 2 * peers, peers)
        m = across(to)
        return jnp.where(m < half, peers - 1 - m, m - half + 1 - 2 * lax.rem(m, 2))

    edge_place = place_of(edge_peer)

    def target(i):
        skipped = jnp.where(i >= edge_place, i + 1, i)
        return rank(jnp.where(i == peers - 1, edge_place, skipped))

    def send_of(to):
        return pltpu.make_async_remote_copy(
            src_ref=sec.at[to],
            dst_ref=got.at[me],
            send_sem=send_sem.at[to],
            recv_sem=recv_sem.at[me],
            device_id={"shot": to},
            device_id_type=MESH,
        )

    def recv_of(origin):
        return pltpu.make_async_remote_copy(
            src_ref=sec.at[origin],
            dst_ref=got.at[origin],
            send_sem=send_sem.at[origin],
            recv_sem=recv_sem.at[origin],
            device_id={"shot": origin},
            device_id_type=MESH,
        )

    def gather(to, sums):
        for c in range(chunks):
            row0 = to * per_peer + c * GROUP
            if per_peer % GROUP == 0:
                row0 = pl.multiple_of(row0, GROUP)
            at = pl.ds(row0, GROUP)
            total0, total1 = [None] * nb, [None] * nb
            for a in range(kr):
                d = r_d[a, at, :]
                source = pl.ds(EDGE - AR + row0 + a, GROUP)
                unit = near_unit[source, :]
                whole = rtaper_ref[a] * unit
                c1 = whole * r_w[a, at, :]
                c0 = whole - c1
                idx, own = (lane + d) & (LANES - 1), lane >= d
                now = near[0, source, :]
                for b in range(pairs):
                    after = near[b + 1, source, :]
                    word = jnp.take_along_axis(jnp.where(own, now, after), idx, axis=1)
                    now = after
                    for n, value in zip((b, b + pairs), unpacked(word)):
                        total0[n] = c0 * value if a == 0 else total0[n] + c0 * value
                        total1[n] = c1 * value if a == 0 else total1[n] + c1 * value
            where = side * rows + row0 + sub
            last = jnp.minimum(jnp.minimum(live_count, rows * n_rcv) - 1, where + AR)
            fold = last - jnp.maximum(where - AR, 0) + 1
            norm = 1.0 / jnp.sqrt(jnp.maximum(fold, 1).astype(f32))
            rows_of = slice(c * GROUP, c * GROUP + GROUP)
            for b in range(nb):
                sums[0][b, rows_of, :] = total0[b] * norm
                sums[1][b, rows_of, :] = total1[b] * norm

    def emit(to, sums):
        later = ahead([sums[1][b].astype(jnp.bfloat16).astype(f32) for b in range(nb)])
        one = [(sums[0][b] + later[b]).astype(jnp.bfloat16).astype(f32) for b in range(nb)]
        for b, value in enumerate(smooth(one)):
            sec[to, :, b * LANES : (b + 1) * LANES] = value[:per_peer]


    def dispatch(to):
        @pl.when(to != me)
        def _():
            send_of(to).start()

        @pl.when(to == me)
        def _():
            got[me] = sec[me]

    even, odd = (sum0, sum1), (sum2, sum3)
    def filter_all():
        lax.fori_loop(0, rows // EDGE, filter_own, 0, unroll=4)

    if per_peer == EDGE:
        for step in (-1, 0, 1):
            filter_own(jnp.minimum(jnp.maximum(target(0) + step, 0), peers - 1), 0)
    else:
        filter_all()
    gather(target(0), even)
    emit(target(0), even)
    def enter():
        pl.semaphore_wait(barrier, peers - 1 + side)

        @pl.when(side == 1)
        def _():
            halo_copy.start()

        dispatch(target(0))

    @pl.when(me >= half)
    def _():
        enter()

    if per_peer == EDGE:
        filter_all()
    if peers > 1:
        gather(target(1), odd)

    @pl.when(me < half)
    def _():
        enter()

    if peers > 1:

        def receiver_steps(n, carry):
            for i, now, then in ((2 * n + 1, odd, even), (2 * n + 2, even, odd)):
                @pl.when(i == peers - 2)
                def _():
                    halo_copy.wait_recv()

                    @pl.when(side == 0)
                    def _():
                        halo_copy.start()

                    filter_rows(
                        lambda b: halo[:, b * LANES : (b + 1) * LANES],
                        pl.multiple_of(other * (EDGE + rows), EDGE),
                    )

                gather(target(i + 1), then)
                emit(target(i), now)
                dispatch(target(i))
            return carry

        lax.fori_loop(0, peers // 2 - 1, receiver_steps, 0)
        emit(target(peers - 1), odd)
        dispatch(target(peers - 1))

    for n in (3, 4, 5):
        loads[n].wait()
    group = LANES // EDGE

    def source_tables(g, carry):
        for kk in range(group):
            for a in range(ks):
                at = kk * EDGE + a
                flat[at : at + 1, :per_peer] = sd_ref[g * group + kk, a] * 256 + sf_ref[g * group + kk, a]
        turned[0] = jnp.transpose(flat[...], (1, 0))
        for kk in range(group):
            k = g * group + kk
            count = jnp.minimum(k + ks - AS, peers) - jnp.maximum(k - AS, 0)
            norm = 1.0 / jnp.sqrt(jnp.full((GROUP, LANES), count, jnp.int32).astype(f32))
            for c in range(chunks):
                at = slice(c * GROUP, c * GROUP + GROUP)
                columns = turned[0, at, :]
                for a in range(ks):
                    if peers == group and not 0 <= kk + a - AS < peers:
                        continue
                    d, weight = spread(columns[:, kk * EDGE + a : kk * EDGE + a + 1])
                    scale = staper_ref[a] * norm
                    t_d[k, a, at, :] = d
                    t_c0[k, a, at, :] = scale * (1.0 - weight)
                    t_c1[k, a, at, :] = scale * weight
        return carry

    lax.fori_loop(0, peers // group, source_tables, 0)

    def clear(k, carry):
        for b in range(nb):
            acc0[k, b] = jnp.zeros(acc0.shape[2:], f32)
            acc1[k, b] = jnp.zeros(acc1.shape[2:], f32)
        return carry

    lax.fori_loop(0, peers, clear, 0)

    if per_peer < GROUP:
        for table in ((far, far_unit), (far1, far1_unit)):
            table[0][...] = jnp.zeros(far.shape, jnp.int32)
            table[1][...] = jnp.zeros(far_unit.shape, f32)
    width = min(peers, ks)

    def prepare(p, table):
        packed, unit = words([got[p, :, b * LANES : (b + 1) * LANES].astype(f32) for b in range(nb)])
        for b, word in enumerate(packed):
            table[0][b, :per_peer, :] = word
        table[1][:per_peer, :] = unit

    def accumulate(p, table):
        base = 0 if width == peers else jnp.minimum(jnp.maximum(p - AS, 0), peers - width)
        for kk in range(width):
            k = base + kk
            tap = p - k + AS
            a = jnp.minimum(jnp.maximum(tap, 0), ks - 1)
            inside = jnp.where(tap == a, 1.0, 0.0)
            for c in range(chunks):
                at = slice(c * GROUP, c * GROUP + GROUP)
                d, unit = t_d[k, a, at, :], table[1][at, :] * inside
                c0, c1 = t_c0[k, a, at, :] * unit, t_c1[k, a, at, :] * unit
                idx, own = (lane + d) & (LANES - 1), lane >= d
                now = table[0][0, at, :]
                for b in range(pairs):
                    after = table[0][b + 1, at, :]
                    word = jnp.take_along_axis(jnp.where(own, now, after), idx, axis=1)
                    now = after
                    for n, value in zip((b, b + pairs), unpacked(word)):
                        acc0[k, n, at, :] += c0 * value
                        acc1[k, n, at, :] += c1 * value

    def arrive(i, table):
        recv_of(source(i)).wait_recv()
        prepare(source(i), table)

    first, second = (far, far_unit), (far1, far1_unit)
    prepare(me, first)

    def source_steps(n, carry):
        arrive(2 * n + 1, second)
        accumulate(source(2 * n), first)
        arrive(2 * n + 2, first)
        accumulate(source(2 * n + 1), second)
        return carry

    if peers > 1:
        lax.fori_loop(0, peers // 2 - 1, source_steps, 0)
        arrive(peers - 1, second)
        accumulate(source(peers - 2), first)
        accumulate(source(peers - 1), second)
    else:
        accumulate(me, first)

    def finish(k, carry):
        later = ahead([acc1[k, b].astype(jnp.bfloat16).astype(f32) for b in range(nb)])
        for b in range(nb):
            value = (acc0[k, b] + later[b]).astype(jnp.bfloat16)
            out_ref[k, 0, :, b * LANES : (b + 1) * LANES] = value[:per_peer]
        return carry

    lax.fori_loop(0, peers, finish, 0, unroll=min(peers, 8))

    halo_copy.wait_send()

    def drain(i, carry):
        send_of(source(i)).wait_send()
        return carry

    lax.fori_loop(1, peers, drain, 0)


def body(traces, rcv_delay, rcv_frac, live_count, src_delay, src_frac, rcv_taper, src_taper):
    _, rows, nt = traces.shape
    peers = lax.axis_size("shot")
    n_rcv = lax.axis_size("rcv")
    per_peer = rows // peers
    kr, ks = rcv_delay.shape[-1], src_delay.shape[-1]
    nb = nt // LANES
    tall = pl.cdiv(per_peer, GROUP) * GROUP
    rcv_delay, rcv_frac = (jnp.transpose(v, (2, 0, 1)) for v in (rcv_delay, rcv_frac))
    src_delay, src_frac = (jnp.transpose(v, (0, 3, 1, 2)) for v in (src_delay, src_frac))
    dims = (rows, nt, peers, per_peer, n_rcv, kr, ks)
    hbm, vmem = pl.BlockSpec(memory_space=pltpu.HBM), pl.BlockSpec(memory_space=pltpu.VMEM)
    keep = functools.partial(pltpu.with_memory_space_constraint, memory_space=pltpu.HBM)
    near = functools.partial(pltpu.with_memory_space_constraint, memory_space=pltpu.VMEM)
    f32, bf16, i32 = jnp.float32, jnp.bfloat16, jnp.int32
    extended = (nb // 2 + 1, rows + 2 * EDGE, LANES)
    r_table = (kr, rows + GROUP, LANES)
    t_table = (peers, ks, tall, LANES)
    return pl.pallas_call(
        functools.partial(kernel, dims),
        name="redatum",
        out_shape=pltpu.VMEM((peers, 1, per_peer, nt), bf16),
        in_specs=[hbm] * 4 + [vmem] * 2 + [hbm] * 2,
        out_specs=pl.BlockSpec(memory_space=pltpu.VMEM),
        scratch_shapes=[
            pltpu.SMEM((1,), i32),
            pltpu.SMEM((kr,), f32),
            pltpu.SMEM((ks,), f32),
            pltpu.VMEM((rows, nt), bf16),
            pltpu.VMEM(src_delay.shape, i32),
            pltpu.VMEM(src_delay.shape, i32),
            pltpu.SemaphoreType.DMA((6,)),
            pltpu.VMEM((LANES, LANES), i32),
            pltpu.VMEM((rows // LANES, LANES, LANES), i32),
            pltpu.VMEM(extended, i32),
            pltpu.VMEM(extended[1:], f32),
            pltpu.VMEM((nb // 2 + 1, tall, LANES), i32),
            pltpu.VMEM((tall, LANES), f32),
            pltpu.VMEM((nb // 2 + 1, tall, LANES), i32),
            pltpu.VMEM((tall, LANES), f32),
            pltpu.VMEM((EDGE, nt), bf16),
            pltpu.VMEM((peers, per_peer, nt), bf16),
            pltpu.VMEM((peers, per_peer, nt), bf16),
            pltpu.VMEM((nb, tall, LANES), f32),
            pltpu.VMEM((nb, tall, LANES), f32),
            pltpu.VMEM((nb, tall, LANES), f32),
            pltpu.VMEM((nb, tall, LANES), f32),
            pltpu.VMEM((peers, nb, tall, LANES), f32),
            pltpu.VMEM((peers, nb, tall, LANES), f32),
            pltpu.VMEM(r_table, i32),
            pltpu.VMEM(r_table, f32),
            pltpu.VMEM(t_table, i32),
            pltpu.VMEM(t_table, f32),
            pltpu.VMEM(t_table, f32),
            pltpu.SemaphoreType.DMA,
            pltpu.SemaphoreType.DMA,
            pltpu.SemaphoreType.DMA((peers,)),
            pltpu.SemaphoreType.DMA((peers,)),
        ],
        compiler_params=pltpu.CompilerParams(
            collective_id=0, has_side_effects=True, vmem_limit_bytes=60 * 2**20
        ),
    )(
        live_count, keep(rcv_taper), keep(src_taper), keep(traces), near(rcv_delay), near(rcv_frac), keep(src_delay), keep(src_frac)
    )


def solution(mesh):
    return jax.shard_map(
        body,
        mesh=mesh,
        in_specs=(
            P(("slab", "shot"), "rcv", None),
            P(("slab", "shot"), "rcv", None),
            P(("slab", "shot"), "rcv", None),
            P(("slab", "shot")),
            P("slab", "rcv", "shot", None),
            P("slab", "rcv", "shot", None),
            P(),
            P(),
        ),
        out_specs=P("slab", "rcv", "shot", None),
        check_vma=False,
    )
```

```python
import functools

import jax
import jax.numpy as jnp
import numpy as np
from jax import lax
from jax.experimental import pallas as pl
from jax.experimental.pallas import tpu as pltpu
from jax.sharding import PartitionSpec as P

AR = 4
AS = 4
TRI = 2
LANES = 128
GROUP = 8
EDGE = 16
FULL = 32000.0
TINY = 1e-30
MESH = pl.DeviceIdType.MESH


def taps_of_filter():
    heights = np.maximum(TRI - np.abs(np.arange(-TRI, TRI + 1)), 0).astype(np.float32)
    taps = (heights / np.sqrt(np.sum(heights**2, dtype=np.float32))).astype(jnp.bfloat16)
    return [float(v) for v in taps[TRI:]]


MAIN_TAP, SIDE_TAP = taps_of_filter()[:2]


def ends(shape):
    lane = lax.broadcasted_iota(jnp.int32, shape, 1)
    return lane == 0, lane == LANES - 1


def smooth(raw):
    is_first, is_last = ends(raw[0].shape)
    zero = jnp.zeros_like(raw[0])
    up = [zero] + [pltpu.roll(x, 1, 1) for x in raw]
    down = [pltpu.roll(x, LANES - 1, 1) for x in raw] + [zero]
    done = []
    for b, x in enumerate(raw):
        before = jnp.where(is_first, up[b], up[b + 1])
        after = jnp.where(is_last, down[b + 1], down[b])
        done.append((MAIN_TAP * x + SIDE_TAP * (before + after)).astype(jnp.bfloat16))
    return done


def ahead(values):
    _, is_last = ends(values[0].shape)
    rolled = [pltpu.roll(x, LANES - 1, 1) for x in values] + [jnp.zeros_like(values[0])]
    return [jnp.where(is_last, rolled[b + 1], rolled[b]) for b in range(len(values))]


def words(values):
    pairs = len(values) // 2
    top = functools.reduce(jnp.maximum, [jnp.abs(v) for v in values])
    top = jnp.maximum(jnp.max(top, axis=1, keepdims=True), TINY)
    top = jnp.broadcast_to(top, values[0].shape)
    scale = FULL / top
    whole = [(v * scale).astype(jnp.int32) for v in values]
    packed = [(whole[b] << 16) + whole[b + pairs] for b in range(pairs)]
    return packed + [whole[pairs] << 16], top * (1.0 / (FULL * 65536.0))


def unpacked(word):
    return word.astype(jnp.float32), (word << 16).astype(jnp.float32)


def kernel(
    dims,
    live_hbm, rtaper_hbm, staper_hbm, x_hbm, rd_ref, rf_ref, sd_hbm, sf_hbm,
    out_ref,
    live_ref, rtaper_ref, staper_ref, x_ref, sd_ref, sf_ref, in_sem,
    flat, band, turned, near, near_unit, far, far_unit, far1, far1_unit, halo, sec, got, sum0, sum1, sum2, sum3, acc0, acc1,
    r_d, r_w, t_d, t_c0, t_c1,
    halo_send, halo_recv, send_sem, recv_sem,
):
    rows, nt, peers, per_peer, n_rcv, kr, ks = dims
    nb = nt // LANES
    pairs = nb // 2
    chunks = pl.cdiv(per_peer, GROUP)
    me = lax.axis_index("shot")
    side = lax.axis_index("rcv")
    other = 1 - side
    f32 = jnp.float32

    copies = (
        (x_hbm.at[0], x_ref), (live_hbm, live_ref), (rtaper_hbm, rtaper_ref),
        (staper_hbm, staper_ref), (sd_hbm, sd_ref), (sf_hbm, sf_ref),
    )
    loads = [pltpu.make_async_copy(a, b, in_sem.at[n]) for n, (a, b) in enumerate(copies)]
    for load in loads:
        load.start()

    barrier = pltpu.get_barrier_semaphore()

    def greet(i, carry):
        to = lax.rem(me + i, peers)
        pl.semaphore_signal(barrier, inc=1, device_id={"shot": to}, device_id_type=MESH)
        return carry

    @pl.when(side == 0)
    def _():
        pl.semaphore_signal(barrier, inc=1, device_id={"rcv": other}, device_id_type=MESH)

    lax.fori_loop(1, peers, greet, 0)

    for start in (0, EDGE + rows):
        for b in range(pairs + 1):
            near[b, start : start + EDGE, :] = jnp.zeros((EDGE, LANES), jnp.int32)
        near_unit[start : start + EDGE, :] = jnp.zeros((EDGE, LANES), f32)
    flat[...] = jnp.zeros_like(flat)

    gap = lax.broadcasted_iota(jnp.int32, band.shape, 0) - lax.broadcasted_iota(jnp.int32, band.shape, 1) - LANES
    near_taps = jnp.where(jnp.abs(gap) == 1, SIDE_TAP, 0.0)
    band[...] = jnp.where(gap == 0, MAIN_TAP, near_taps).astype(jnp.bfloat16)

    lane = lax.broadcasted_iota(jnp.int32, (GROUP, LANES), 1)
    sub = lax.broadcasted_iota(jnp.int32, (GROUP, LANES), 0)

    def spread(column):
        packed = jnp.broadcast_to(column, (GROUP, LANES))
        return packed >> 8, (packed & 255).astype(f32) * (1.0 / 256.0)

    for block in range(rows // LANES):
        cols = slice(block * LANES, (block + 1) * LANES)
        for a in range(kr):
            flat[a : a + 1, :] = rd_ref[a, :, cols] * 256 + rf_ref[a, :, cols]
        turned[block] = jnp.transpose(flat[...], (1, 0))

    def receiver_tables(g, carry):
        at = pl.ds(pl.multiple_of(g * GROUP, GROUP), GROUP)
        columns = turned[g // (LANES // GROUP), pl.ds(pl.multiple_of(lax.rem(g, LANES // GROUP) * GROUP, GROUP), GROUP), :]
        for a in range(kr):
            d, weight = spread(columns[:, a : a + 1])
            r_d[a, at, :] = d
            r_w[a, at, :] = weight
        return carry

    lax.fori_loop(0, rows // GROUP, receiver_tables, 0, unroll=4)

    halo_copy = pltpu.make_async_remote_copy(
        src_ref=x_hbm.at[0, pl.ds(pl.multiple_of(other * (rows - EDGE), EDGE), EDGE), :],
        dst_ref=halo,
        send_sem=halo_send,
        recv_sem=halo_recv,
        device_id={"rcv": other},
        device_id_type=MESH,
    )

    def filter_rows(load, base):
        done = [v.astype(f32) for v in smooth([load(b).astype(f32) for b in range(nb)])]
        packed, unit = words(done)
        where = side * rows + base - EDGE + lax.broadcasted_iota(jnp.int32, (EDGE, LANES), 0)
        unit = jnp.where(where < live_count, unit, 0.0)
        for b, word in enumerate(packed):
            near[b, pl.ds(base, EDGE), :] = word
        near_unit[pl.ds(base, EDGE), :] = unit

    def filter_own(g, carry):
        start = pl.multiple_of(g * EDGE, EDGE)
        filter_rows(lambda b: x_ref[pl.ds(start, EDGE), b * LANES : (b + 1) * LANES], EDGE + start)
        return carry

    for n in range(3):
        loads[n].wait()
    live_count = live_ref[0]

    edge_peer = other * (peers - 1)

    half = max(peers // 2, 1)

    def across(m):
        total, unit = 0, 1
        while unit < peers:
            x, y = lax.rem(me // unit, 2), lax.rem(m // unit, 2)
            total = total + unit * (x + y - 2 * x * y)
            unit *= 2
        return total

    def partner(m, i):
        return across(m) if peers & (peers - 1) == 0 else lax.rem(me + i, peers)

    def source(i):
        far_half = half + (i - half) + 1 - 2 * lax.rem(i, 2)
        return partner(jnp.where(i == 0, 0, jnp.where(i < half, half - i, far_half)), i)

    def rank(i):
        return partner(jnp.where(i < half, half + i + 1 - 2 * lax.rem(i, 2), peers - 1 - i), i + 1)

    def place_of(to):
        if peers & (peers - 1):
            return lax.rem(to - me - 1 + 2 * peers, peers)
        m = across(to)
        return jnp.where(m < half, peers - 1 - m, m - half + 1 - 2 * lax.rem(m, 2))

    edge_place = place_of(edge_peer)

    def target(i):
        skipped = jnp.where(i >= edge_place, i + 1, i)
        return rank(jnp.where(i == peers - 1, edge_place, skipped))

    def send_of(to):
        return pltpu.make_async_remote_copy(
            src_ref=sec.at[to],
            dst_ref=got.at[me],
            send_sem=send_sem.at[to],
            recv_sem=recv_sem.at[me],
            device_id={"shot": to},
            device_id_type=MESH,
        )

    def recv_of(origin):
        return pltpu.make_async_remote_copy(
            src_ref=sec.at[origin],
            dst_ref=got.at[origin],
            send_sem=send_sem.at[origin],
            recv_sem=recv_sem.at[origin],
            device_id={"shot": origin},
            device_id_type=MESH,
        )

    def gather(to, sums):
        for c in range(chunks):
            row0 = to * per_peer + c * GROUP
            if per_peer % GROUP == 0:
                row0 = pl.multiple_of(row0, GROUP)
            at = pl.ds(row0, GROUP)
            total0, total1 = [None] * nb, [None] * nb
            for a in range(kr):
                d = r_d[a, at, :]
                source = pl.ds(EDGE - AR + row0 + a, GROUP)
                unit = near_unit[source, :]
                whole = rtaper_ref[a] * unit
                c1 = whole * r_w[a, at, :]
                c0 = whole - c1
                idx, own = (lane + d) & (LANES - 1), lane >= d
                now = near[0, source, :]
                for b in range(pairs):
                    after = near[b + 1, source, :]
                    word = jnp.take_along_axis(jnp.where(own, now, after), idx, axis=1)
                    now = after
                    for n, value in zip((b, b + pairs), unpacked(word)):
                        total0[n] = c0 * value if a == 0 else total0[n] + c0 * value
                        total1[n] = c1 * value if a == 0 else total1[n] + c1 * value
            where = side * rows + row0 + sub
            last = jnp.minimum(jnp.minimum(live_count, rows * n_rcv) - 1, where + AR)
            fold = last - jnp.maximum(where - AR, 0) + 1
            norm = 1.0 / jnp.sqrt(jnp.maximum(fold, 1).astype(f32))
            rows_of = slice(c * GROUP, c * GROUP + GROUP)
            for b in range(nb):
                sums[0][b, rows_of, :] = total0[b] * norm
                sums[1][b, rows_of, :] = total1[b] * norm

    def emit(to, sums):
        later = ahead([sums[1][b].astype(jnp.bfloat16).astype(f32) for b in range(nb)])
        one = [(sums[0][b] + later[b]).astype(jnp.bfloat16).astype(f32) for b in range(nb)]
        if per_peer % EDGE == 0:
            blank = jnp.zeros(one[0].shape, jnp.bfloat16)
            padded = [blank] + [v.astype(jnp.bfloat16) for v in one] + [blank]
            wide = [jnp.concatenate(padded[b : b + 3], axis=1) for b in range(nb)]
            flat_out = jnp.dot(jnp.concatenate(wide, axis=0), band[...], preferred_element_type=f32)
            done = [flat_out[b * per_peer : (b + 1) * per_peer].astype(jnp.bfloat16) for b in range(nb)]
        else:
            done = smooth(one)
        for b, value in enumerate(done):
            sec[to, :, b * LANES : (b + 1) * LANES] = value[:per_peer]


    def dispatch(to):
        @pl.when(to != me)
        def _():
            send_of(to).start()

        @pl.when(to == me)
        def _():
            got[me] = sec[me]

    even, odd = (sum0, sum1), (sum2, sum3)
    def filter_all():
        lax.fori_loop(0, rows // EDGE, filter_own, 0, unroll=4)

    if per_peer == EDGE:
        for step in (-1, 0, 1):
            filter_own(jnp.minimum(jnp.maximum(target(0) + step, 0), peers - 1), 0)
    else:
        filter_all()
    gather(target(0), even)
    emit(target(0), even)
    def enter():
        pl.semaphore_wait(barrier, peers - 1 + side)

        @pl.when(side == 1)
        def _():
            halo_copy.start()

        dispatch(target(0))

    @pl.when(me >= half)
    def _():
        enter()

    if per_peer == EDGE:
        filter_all()
    if peers > 1:
        gather(target(1), odd)

    @pl.when(me < half)
    def _():
        enter()

    if peers > 1:

        def receiver_steps(n, carry):
            for i, now, then in ((2 * n + 1, odd, even), (2 * n + 2, even, odd)):
                @pl.when(i == peers - 2)
                def _():
                    halo_copy.wait_recv()

                    @pl.when(side == 0)
                    def _():
                        halo_copy.start()

                    filter_rows(
                        lambda b: halo[:, b * LANES : (b + 1) * LANES],
                        pl.multiple_of(other * (EDGE + rows), EDGE),
                    )

                gather(target(i + 1), then)
                emit(target(i), now)
                dispatch(target(i))
            return carry

        lax.fori_loop(0, peers // 2 - 1, receiver_steps, 0)
        emit(target(peers - 1), odd)
        dispatch(target(peers - 1))

    for n in (3, 4, 5):
        loads[n].wait()
    group = LANES // EDGE

    def source_tables(g, carry):
        for kk in range(group):
            for a in range(ks):
                at = kk * EDGE + a
                flat[at : at + 1, :per_peer] = sd_ref[g * group + kk, a] * 256 + sf_ref[g * group + kk, a]
        turned[0] = jnp.transpose(flat[...], (1, 0))
        for kk in range(group):
            k = g * group + kk
            count = jnp.minimum(k + ks - AS, peers) - jnp.maximum(k - AS, 0)
            norm = 1.0 / jnp.sqrt(jnp.full((GROUP, LANES), count, jnp.int32).astype(f32))
            for c in range(chunks):
                at = slice(c * GROUP, c * GROUP + GROUP)
                columns = turned[0, at, :]
                for a in range(ks):
                    if peers == group and not 0 <= kk + a - AS < peers:
                        continue
                    d, weight = spread(columns[:, kk * EDGE + a : kk * EDGE + a + 1])
                    scale = staper_ref[a] * norm
                    t_d[k, a, at, :] = d
                    t_c0[k, a, at, :] = scale * (1.0 - weight)
                    t_c1[k, a, at, :] = scale * weight
        return carry

    lax.fori_loop(0, peers // group, source_tables, 0)

    def clear(k, carry):
        for b in range(nb):
            acc0[k, b] = jnp.zeros(acc0.shape[2:], f32)
            acc1[k, b] = jnp.zeros(acc1.shape[2:], f32)
        return carry

    lax.fori_loop(0, peers, clear, 0)

    if per_peer < GROUP:
        for table in ((far, far_unit), (far1, far1_unit)):
            table[0][...] = jnp.zeros(far.shape, jnp.int32)
            table[1][...] = jnp.zeros(far_unit.shape, f32)
    width = min(peers, ks)

    def prepare(p, table):
        packed, unit = words([got[p, :, b * LANES : (b + 1) * LANES].astype(f32) for b in range(nb)])
        for b, word in enumerate(packed):
            table[0][b, :per_peer, :] = word
        table[1][:per_peer, :] = unit

    def accumulate(p, table):
        base = 0 if width == peers else jnp.minimum(jnp.maximum(p - AS, 0), peers - width)
        for kk in range(width):
            k = base + kk
            tap = p - k + AS
            a = jnp.minimum(jnp.maximum(tap, 0), ks - 1)
            inside = jnp.where(tap == a, 1.0, 0.0)
            for c in range(chunks):
                at = slice(c * GROUP, c * GROUP + GROUP)
                d, unit = t_d[k, a, at, :], table[1][at, :] * inside
                c0, c1 = t_c0[k, a, at, :] * unit, t_c1[k, a, at, :] * unit
                idx, own = (lane + d) & (LANES - 1), lane >= d
                now = table[0][0, at, :]
                for b in range(pairs):
                    after = table[0][b + 1, at, :]
                    word = jnp.take_along_axis(jnp.where(own, now, after), idx, axis=1)
                    now = after
                    for n, value in zip((b, b + pairs), unpacked(word)):
                        acc0[k, n, at, :] += c0 * value
                        acc1[k, n, at, :] += c1 * value

    def arrive(i, table):
        recv_of(source(i)).wait_recv()
        prepare(source(i), table)

    first, second = (far, far_unit), (far1, far1_unit)
    prepare(me, first)

    def source_steps(n, carry):
        arrive(2 * n + 1, second)
        accumulate(source(2 * n), first)
        arrive(2 * n + 2, first)
        accumulate(source(2 * n + 1), second)
        return carry

    if peers > 1:
        lax.fori_loop(0, peers // 2 - 1, source_steps, 0)
        arrive(peers - 1, second)
        accumulate(source(peers - 2), first)
        accumulate(source(peers - 1), second)
    else:
        accumulate(me, first)

    def finish(k, carry):
        later = ahead([acc1[k, b].astype(jnp.bfloat16).astype(f32) for b in range(nb)])
        for b in range(nb):
            value = (acc0[k, b] + later[b]).astype(jnp.bfloat16)
            out_ref[k, 0, :, b * LANES : (b + 1) * LANES] = value[:per_peer]
        return carry

    lax.fori_loop(0, peers, finish, 0, unroll=min(peers, 8))

    halo_copy.wait_send()

    def drain(i, carry):
        send_of(source(i)).wait_send()
        return carry

    lax.fori_loop(1, peers, drain, 0)


def body(traces, rcv_delay, rcv_frac, live_count, src_delay, src_frac, rcv_taper, src_taper):
    _, rows, nt = traces.shape
    peers = lax.axis_size("shot")
    n_rcv = lax.axis_size("rcv")
    per_peer = rows // peers
    kr, ks = rcv_delay.shape[-1], src_delay.shape[-1]
    nb = nt // LANES
    tall = pl.cdiv(per_peer, GROUP) * GROUP
    rcv_delay, rcv_frac = (jnp.transpose(v, (2, 0, 1)) for v in (rcv_delay, rcv_frac))
    src_delay, src_frac = (jnp.transpose(v, (0, 3, 1, 2)) for v in (src_delay, src_frac))
    dims = (rows, nt, peers, per_peer, n_rcv, kr, ks)
    hbm, vmem = pl.BlockSpec(memory_space=pltpu.HBM), pl.BlockSpec(memory_space=pltpu.VMEM)
    keep = functools.partial(pltpu.with_memory_space_constraint, memory_space=pltpu.HBM)
    near = functools.partial(pltpu.with_memory_space_constraint, memory_space=pltpu.VMEM)
    f32, bf16, i32 = jnp.float32, jnp.bfloat16, jnp.int32
    extended = (nb // 2 + 1, rows + 2 * EDGE, LANES)
    r_table = (kr, rows + GROUP, LANES)
    t_table = (peers, ks, tall, LANES)
    return pl.pallas_call(
        functools.partial(kernel, dims),
        name="redatum",
        out_shape=pltpu.VMEM((peers, 1, per_peer, nt), bf16),
        in_specs=[hbm] * 4 + [vmem] * 2 + [hbm] * 2,
        out_specs=pl.BlockSpec(memory_space=pltpu.VMEM),
        scratch_shapes=[
            pltpu.SMEM((1,), i32),
            pltpu.SMEM((kr,), f32),
            pltpu.SMEM((ks,), f32),
            pltpu.VMEM((rows, nt), bf16),
            pltpu.VMEM(src_delay.shape, i32),
            pltpu.VMEM(src_delay.shape, i32),
            pltpu.SemaphoreType.DMA((6,)),
            pltpu.VMEM((LANES, LANES), i32),
            pltpu.VMEM((3 * LANES, LANES), bf16),
            pltpu.VMEM((rows // LANES, LANES, LANES), i32),
            pltpu.VMEM(extended, i32),
            pltpu.VMEM(extended[1:], f32),
            pltpu.VMEM((nb // 2 + 1, tall, LANES), i32),
            pltpu.VMEM((tall, LANES), f32),
            pltpu.VMEM((nb // 2 + 1, tall, LANES), i32),
            pltpu.VMEM((tall, LANES), f32),
            pltpu.VMEM((EDGE, nt), bf16),
            pltpu.VMEM((peers, per_peer, nt), bf16),
            pltpu.VMEM((peers, per_peer, nt), bf16),
            pltpu.VMEM((nb, tall, LANES), f32),
            pltpu.VMEM((nb, tall, LANES), f32),
            pltpu.VMEM((nb, tall, LANES), f32),
            pltpu.VMEM((nb, tall, LANES), f32),
            pltpu.VMEM((peers, nb, tall, LANES), f32),
            pltpu.VMEM((peers, nb, tall, LANES), f32),
            pltpu.VMEM(r_table, i32),
            pltpu.VMEM(r_table, f32),
            pltpu.VMEM(t_table, i32),
            pltpu.VMEM(t_table, f32),
            pltpu.VMEM(t_table, f32),
            pltpu.SemaphoreType.DMA,
            pltpu.SemaphoreType.DMA,
            pltpu.SemaphoreType.DMA((peers,)),
            pltpu.SemaphoreType.DMA((peers,)),
        ],
        compiler_params=pltpu.CompilerParams(
            collective_id=0, has_side_effects=True, vmem_limit_bytes=60 * 2**20
        ),
    )(
        live_count, keep(rcv_taper), keep(src_taper), keep(traces), near(rcv_delay), near(rcv_frac), keep(src_delay), keep(src_frac)
    )


def solution(mesh):
    return jax.shard_map(
        body,
        mesh=mesh,
        in_specs=(
            P(("slab", "shot"), "rcv", None),
            P(("slab", "shot"), "rcv", None),
            P(("slab", "shot"), "rcv", None),
            P(("slab", "shot")),
            P("slab", "rcv", "shot", None),
            P("slab", "rcv", "shot", None),
            P(),
            P(),
        ),
        out_specs=P("slab", "rcv", "shot", None),
        check_vma=False,
    )
```
